32 devices in a mesh: grp: 8 (over z, y), row: 4 (over x, core).
Axes of the slice: x: 2, y: 2, z: 4, core: 2. Of those that a mesh axis runs over, the one named last changes fastest.
Arguments:
- view_a: float32 [4096, 8192], P('row', 'grp'), may hold values from -40 to 40
- view_b: float32 [4096, 8192], P('row', 'grp'), may hold values from -40 to 40
Outputs:
- grad_a: float32 [4096, 8192], P('row', 'grp')
- grad_b: float32 [4096, 8192], P('row', 'grp')
The draws below stay inside these ranges and needn't reach their ends.
All inputs are finite; a program needn't handle non-finite values.
Results may differ from the reference program's by a relative error of at most 0.00025.
Values sent between devices are 32-bit elements; how exact they have to be, the bound alone decides.
A program may use at most 128 MiB of HBM per device.

```python
import jax
import jax.numpy as jnp
from jax import lax

F = 8192
NROWS = 4096
N_GRP = 8


def make_views(key):
    keys = jax.random.split(jax.random.fold_in(key, 7), 4)
    base_part = jax.random.normal(keys[0], (NROWS, F), jnp.float32)
    common = jax.random.normal(keys[1], (NROWS, 1), jnp.float32)
    direction = jax.random.normal(keys[2], (1, F), jnp.float32)
    noise_part = jax.random.normal(keys[3], (NROWS, F), jnp.float32)
    first = base_part + 0.4 * common * direction
    second = 0.8 * first + 0.6 * noise_part
    return (jnp.clip(first, -40.0, 40.0), jnp.clip(second, -40.0, 40.0))


def draw_view_a(key, part):
    return make_views(key)[0]


def draw_view_b(key, part):
    return make_views(key)[1]


def setup_inputs(seed: int = 0) -> dict:
    splits = jax.random.split(jax.random.key(seed), 3)
    return {
        "view_a": draw_view_a(jax.random.fold_in(splits[2], 71), 0),
        "view_b": draw_view_b(jax.random.fold_in(splits[2], 71), 0),
    }


epsilon = 1e-05
off_weight = 0.0051

def normalize(view):
    mean_val = lax.optimization_barrier(jnp.sum(view, axis=0)) / NROWS
    square = lax.optimization_barrier(jnp.sum(view * view, axis=0)) / NROWS
    scale_val = jnp.sqrt(square - mean_val * mean_val + epsilon)
    return ((view - mean_val) / scale_val, scale_val)

def penalty_of(corr, row_offset, panel_width):
    row_index = row_offset + lax.iota(jnp.int32, corr.shape[0])[:, None]
    column = lax.iota(jnp.int32, corr.shape[1])[None, :]
    on_diagonal = column == row_index + panel_width
    return jnp.where(on_diagonal, -2.0 * (1.0 - corr), 2.0 * off_weight * corr)

def finish(grad, normed, scale_val):
    mean_grad = lax.optimization_barrier(jnp.sum(grad, axis=0)) / NROWS
    mean_cross = lax.optimization_barrier(jnp.sum(grad * normed, axis=0)) / NROWS
    return (grad - mean_grad - normed * mean_cross) / scale_val

def reference(view_a, view_b):
    highest = lax.Precision.HIGHEST
    norm_a, scale_a = normalize(view_a)
    norm_b, scale_b = normalize(view_b)
    panel_width = F // N_GRP
    panels_a = norm_a.reshape(NROWS, N_GRP, panel_width).transpose(1, 0, 2)
    panels_b = norm_b.reshape(NROWS, N_GRP, panel_width).transpose(1, 0, 2)
    neighbours = jnp.concatenate([jnp.roll(panels_b, 1, axis=0), panels_b, jnp.roll(panels_b, -1, axis=0)], axis=2)

    def one_group(pair):
        own, near = pair
        corr = jnp.dot(own.T, near, precision=highest, preferred_element_type=jnp.float32) / NROWS
        penalty = penalty_of(corr, 0, panel_width)
        grad_own = jnp.dot(near, penalty.T, precision=highest, preferred_element_type=jnp.float32)
        contrib = jnp.dot(own, penalty, precision=highest, preferred_element_type=jnp.float32)
        return (grad_own, contrib)
    grad_panels, contribs = lax.map(one_group, (panels_a, neighbours))
    left_part = contribs[:, :, :panel_width]
    middle_part = contribs[:, :, panel_width:2 * panel_width]
    right_part = contribs[:, :, 2 * panel_width:]
    grad_b_panels = middle_part + jnp.roll(left_part, -1, axis=0) + jnp.roll(right_part, 1, axis=0)
    grad_a_full = grad_panels.transpose(1, 0, 2).reshape(NROWS, F)
    grad_b_full = grad_b_panels.transpose(1, 0, 2).reshape(NROWS, F)
    return (finish(grad_a_full, norm_a, scale_a), finish(grad_b_full, norm_b, scale_b))
```

```python
import functools

import jax
import jax.numpy as jnp
from jax import lax
from jax.experimental import pallas as pl
from jax.experimental.pallas import tpu as pltpu
from jax.sharding import PartitionSpec as P

epsilon = 1e-05
off_weight = 0.0051
LANES = 128
SUBLANES = 8
HALVES = 2
PARTS = 4
BLOCK = 256
MESH = pl.DeviceIdType.MESH


def split(block):
    high = block.astype(jnp.bfloat16)
    return high, (block - high.astype(jnp.float32)).astype(jnp.bfloat16)


def dot3(left_high, left_low, right_high, right_low, contract):
    def one(left, right):
        return lax.dot_general(
            left, right, (contract, ((), ())), preferred_element_type=jnp.float32
        )

    cross = one(left_high, right_low) + one(left_low, right_high)
    return cross + one(left_high, right_high)


def kernel(
    groups,
    row_devices,
    view_a,
    view_b,
    ga_out,
    gb_out,
    totals_out,
    ends_out,
    a_high,
    a_low,
    at_high,
    at_low,
    raw,
    own_raw,
    ga,
    back_in,
    swap_in,
    pen,
    share_send,
    share_kept,
    share_in,
    block_high,
    block_low,
    pen_high,
    pen_low,
    stats,
    sums,
    sums_in,
    swap_send_sem,
    swap_recv_sem,
    hop_send_sem,
    hop_recv_sem,
    back_send_sem,
    back_recv_sem,
    home_send_sem,
    home_recv_sem,
    share_send_sem,
    share_recv_sem,
    pen_send_sem,
    pen_recv_sem,
    stat_sem,
    sums_send_sem,
    sums_recv_sem,
    load_sem,
    store_sem,
):
    rows, width = a_high.shape
    chunks = width // LANES
    own_jobs = chunks // 2
    jobs = own_jobs + chunks
    bits = row_devices.bit_length() - 1
    slots = bits + 1
    batch = rows * row_devices
    pair = 2 * LANES
    half_rows = rows // HALVES
    part_rows = rows // PARTS

    group = lax.axis_index("grp")
    row = lax.axis_index("row")
    sign = 1 - 2 * lax.rem(group, 2)
    near = (group + sign, row)
    ahead = (lax.rem(group + groups + 2 * sign, groups), row)
    behind = (lax.rem(group + groups - 2 * sign, groups), row)
    digit = [lax.rem(lax.div(row, 1 << b), 2) for b in range(bits)]
    peer = [(group, row + (1 - 2 * digit[b]) * (1 << b)) for b in range(bits)]
    size = [width >> (b + 1) for b in range(bits)]
    start = [0]
    for b in range(bits):
        start.append(start[b] + digit[b] * size[b])
    away = [start[b] + (1 - digit[b]) * size[b] for b in range(bits)]
    share = size[-1]

    barrier = pltpu.get_barrier_semaphore()
    for device in [near, ahead, behind] + peer:
        pl.semaphore_signal(barrier, inc=1, device_id=device, device_id_type=MESH)
    pl.semaphore_wait(barrier, 3 + bits)

    def remote(source, target, send, recv, device):
        return pltpu.make_async_remote_copy(
            src_ref=source,
            dst_ref=target,
            send_sem=send,
            recv_sem=recv,
            device_id=device,
            device_id_type=MESH,
        )

    def lanes_of(chunk):
        return pl.ds(pl.multiple_of(chunk * LANES, LANES), LANES)

    def swap_copy(chunk, half):
        at = pl.ds(half * half_rows, half_rows)
        return remote(
            view_b.at[at, lanes_of(chunk)],
            raw.at[chunks + chunk, at, :],
            swap_send_sem.at[chunk, half],
            swap_recv_sem.at[chunk, half],
            near,
        )

    def hop_copy(chunk, half):
        at = pl.ds(half * half_rows, half_rows)
        return remote(
            raw.at[chunks + chunk, at, :],
            raw.at[2 * chunks + chunk, at, :],
            hop_send_sem.at[chunk, half],
            hop_recv_sem.at[chunk, half],
            ahead,
        )

    def back_copy(chunk, part):
        at = pl.ds(pl.multiple_of(part * part_rows, part_rows), part_rows)
        return remote(
            raw.at[2 * chunks + chunk, at, :],
            back_in.at[chunk, at, :],
            back_send_sem.at[chunk, part],
            back_recv_sem.at[chunk, part],
            behind,
        )

    def home_copy(chunk, part):
        at = pl.ds(pl.multiple_of(part * part_rows, part_rows), part_rows)
        return remote(
            raw.at[chunks + chunk, at, :],
            swap_in.at[chunk, at, :],
            home_send_sem.at[chunk, part],
            home_recv_sem.at[chunk, part],
            near,
        )

    def share_copy(job, b):
        if b == 0:
            source = share_send.at[lax.rem(job, 2)]
        else:
            at = pl.ds(pl.multiple_of(away[b] - start[b], size[b]), size[b])
            source = share_in[b - 1].at[lax.rem(job, slots), at, :]
        return remote(
            source,
            share_in[b].at[lax.rem(job, slots)],
            share_send_sem.at[b, job],
            share_recv_sem.at[b, job],
            peer[b],
        )

    def pen_copy(job, b):
        at = pl.ds(pl.multiple_of(start[b + 1], size[b]), size[b])
        return remote(
            pen.at[lax.rem(job, slots), at, :],
            pen.at[lax.rem(job, slots), at, :],
            pen_send_sem.at[b, job],
            pen_recv_sem.at[b, job],
            peer[b],
        )

    def sums_copy(which, b):
        return remote(
            sums.at[which, b],
            sums_in.at[which, b],
            sums_send_sem.at[which, b],
            sums_recv_sem.at[which, b],
            peer[b],
        )

    def all_sums(which, between):
        for b in range(bits):
            sums_copy(which, b).start()
            between(b)
            sums_copy(which, b).wait()
            sums[which, b + 1] = sums[which, b] + sums_in[which, b]
        return sums[which, bits]

    def stat_near():
        return remote(
            stats.at[pl.ds(0, chunks)],
            stats.at[pl.ds(chunks, chunks)],
            stat_sem.at[0],
            stat_sem.at[1],
            near,
        )

    def stat_ahead():
        return remote(
            stats.at[pl.ds(chunks, chunks)],
            stats.at[pl.ds(2 * chunks, chunks)],
            stat_sem.at[2],
            stat_sem.at[3],
            ahead,
        )

    load_a = pltpu.make_async_copy(view_a, ga, load_sem.at[0])
    load_a.start()

    def load_own(chunk):
        return pltpu.make_async_copy(
            view_b.at[:, lanes_of(chunk)], own_raw.at[chunk], load_sem.at[1 + chunk]
        )

    for chunk in range(chunks):
        load_own(chunk).start()
    for chunk in range(chunks):
        for half in range(HALVES):
            swap_copy(chunk, half).start()
    load_a.wait()

    def folded(block):
        return jnp.sum(block.reshape(-1, SUBLANES, block.shape[-1]), axis=0)

    def add_a(step, carry):
        at = pl.ds(pl.multiple_of(step * LANES, LANES), LANES)
        block = ga[at, :]
        return carry[0] + folded(block), carry[1] + folded(block * block)

    zero = jnp.zeros((SUBLANES, width), jnp.float32)
    first, second = lax.fori_loop(0, rows // LANES, add_a, (zero, zero))
    sums[0, 0] = zero
    sums[0, 0, 0:1, :] = jnp.sum(first, axis=0, keepdims=True)
    sums[0, 0, 1:2, :] = jnp.sum(second, axis=0, keepdims=True)
    for chunk in range(chunks):
        load_own(chunk).wait()
        block = own_raw[chunk]
        raw[chunk] = block
        at = pl.ds(chunk * LANES, LANES)
        sums[0, 0, 2:3, at] = jnp.sum(folded(block), axis=0, keepdims=True)
        sums[0, 0, 3:4, at] = jnp.sum(folded(block * block), axis=0, keepdims=True)

    def relay(chunk, half):
        swap_copy(chunk, half).wait_recv()
        hop_copy(chunk, half).start()

    totals = all_sums(0, lambda b: None)
    totals_out[...] = totals

    def mean_and_inverse(total, square):
        mean = total / batch
        scale = jnp.sqrt(square / batch - mean * mean + epsilon)
        return mean, 1.0 / scale

    mean_a, inverse_a = mean_and_inverse(totals[0:1, :], totals[1:2, :])
    mean_b, inverse_b = mean_and_inverse(totals[2:3, :], totals[3:4, :])
    for chunk in range(chunks):
        at = slice(chunk * LANES, (chunk + 1) * LANES)
        stats[chunk] = jnp.zeros((SUBLANES, LANES), jnp.float32)
        stats[chunk, 0:1, :] = mean_b[:, at]
        stats[chunk, 1:2, :] = inverse_b[:, at]
    stat_near().start()

    def norm_a(step, carry):
        at = pl.ds(pl.multiple_of(step * LANES, LANES), LANES)
        block = (ga[at, :] - mean_a) * inverse_a
        a_high[at, :], a_low[at, :] = split(block)
        at_high[:, at], at_low[:, at] = split(block.T)
        ga[at, :] = jnp.zeros_like(block)
        return carry

    lax.fori_loop(0, rows // LANES // 2, norm_a, 0)
    relay(0, 0)
    lax.fori_loop(rows // LANES // 2, rows // LANES, norm_a, 0)
    stat_near().wait_recv()
    stat_ahead().start()
    for half in range(1, HALVES):
        relay(0, half)

    def places(job):
        is_own = job < own_jobs
        chunk = job - own_jobs
        first = jnp.where(is_own, 2 * job, chunks + chunk)
        second = jnp.where(is_own, 2 * job + 1, 2 * chunks + chunk)
        return first, second

    def load_block(job):
        for part, place in enumerate(places(job)):
            mean = stats[place, 0:1, :]
            inverse = stats[place, 1:2, :]
            high, low = split((raw[place] - mean) * inverse)
            at = slice(part * LANES, (part + 1) * LANES)
            block_high[:, at] = high
            block_low[:, at] = low

    def correlate(job):
        @pl.when(job >= own_jobs)
        def _():
            @pl.when(job == own_jobs)
            def _():
                stat_ahead().wait_recv()

            for half in range(HALVES):
                hop_copy(job - own_jobs, half).wait_recv()

        load_block(job)

        def part_of(target, base):
            count = min(BLOCK, size[0])

            def body(step, carry):
                offset = pl.multiple_of(step * count, count)
                at = pl.ds(pl.multiple_of(base + offset, count), count)
                target[pl.ds(offset, count), :] = dot3(
                    at_high[at, :],
                    at_low[at, :],
                    block_high[...],
                    block_low[...],
                    ((1,), (0,)),
                ) * (1.0 / batch)
                return carry

            lax.fori_loop(0, size[0] // count, body, 0)

        part_of(share_send.at[lax.rem(job, 2)], away[0])
        share_copy(job, 0).start()
        part_of(share_kept, start[1])

    def reduce_step(job, b):
        share_copy(job, b).wait()
        slot = lax.rem(job, slots)
        if b == 0:
            kept = share_kept[...]
        else:
            at = pl.ds(pl.multiple_of(start[b + 1] - start[b], size[b]), size[b])
            kept = share_in[b - 1][slot, at, :]
        total = kept + share_in[b][slot]
        if b < bits - 1:
            share_in[b][slot] = total
            share_copy(job, b + 1).start()
            return
        shape = (share, pair)
        row_index = start[bits] + lax.broadcasted_iota(jnp.int32, shape, 0)
        base = jnp.where(job < own_jobs, job * pair, -width)
        column = base + lax.broadcasted_iota(jnp.int32, shape, 1)
        value = jnp.where(
            column == row_index, -2.0 * (1.0 - total), 2.0 * off_weight * total
        )
        at = pl.ds(pl.multiple_of(start[bits], share), share)
        pen[slot, at, :] = value
        pen_copy(job, bits - 1).start()

    def gather_step(job, b):
        pen_copy(job, b).wait()
        pen_copy(job, b - 1).start()

    def consume(job):
        pen_copy(job, 0).wait()
        slot = lax.rem(job, slots)
        pen_high[...], pen_low[...] = split(pen[slot])
        load_block(job)
        first, second = places(job)

        @pl.when(job >= own_jobs)
        def _():
            for half in range(HALVES):
                hop_copy(job - own_jobs, half).wait_send()

        def contribute(step, carry):
            at = pl.ds(pl.multiple_of(step * BLOCK, BLOCK), BLOCK)
            value = dot3(
                a_high[at, :], a_low[at, :], pen_high[...], pen_low[...], ((1,), (0,))
            )
            raw[first, at, :] = value[:, :LANES]
            raw[second, at, :] = value[:, LANES:]
            return carry

        lax.fori_loop(0, rows // BLOCK, contribute, 0)

        @pl.when(job >= own_jobs)
        def _():
            for part in range(PARTS):
                back_copy(job - own_jobs, part).start()

        def accumulate(step, carry):
            at = pl.ds(pl.multiple_of(step * BLOCK, BLOCK), BLOCK)
            ga[at, :] += dot3(
                block_high[at, :],
                block_low[at, :],
                pen_high[...],
                pen_low[...],
                ((1,), (1,)),
            )
            return carry

        lax.fori_loop(0, rows // BLOCK, accumulate, 0)

    def step_of(job, k):
        if k <= bits:
            reduce_step(job, k - 1)
        else:
            gather_step(job, 2 * bits - k)

    def send_home(chunk):
        def body(part, carry):
            back_copy(chunk, part).wait_recv()
            at = pl.ds(pl.multiple_of(part * part_rows, part_rows), part_rows)
            raw[chunks + chunk, at, :] += back_in[chunk, at, :]
            home_copy(chunk, part).start()
            return carry

        lax.fori_loop(0, PARTS, body, 0)

    def tick(t, carry):
        following = t - own_jobs + 1
        relays = jnp.logical_and(following >= 1, following < chunks)

        @pl.when(relays)
        def _():
            relay(following, 0)

        def run(job, action):
            pl.when(jnp.logical_and(job >= 0, job < jobs))(lambda: action(job))

        for k in range(2 * bits - 2, 0, -2):
            run(t - k // 2, functools.partial(step_of, k=k))
        run(t, correlate)

        @pl.when(relays)
        def _():
            for half in range(1, HALVES):
                relay(following, half)

        run(t - bits, consume)
        for k in range(1, 2 * bits, 2):
            run(t - k // 2, functools.partial(step_of, k=k))
        home = t - own_jobs - bits - 1

        @pl.when(jnp.logical_and(home >= 0, home < chunks))
        def _():
            send_home(home)

        return carry

    lax.fori_loop(0, jobs + bits + 1, tick, 0)

    def store_a():
        return pltpu.make_async_copy(ga, ga_out, store_sem.at[0])

    def store_b(chunk):
        return pltpu.make_async_copy(
            raw.at[chunk], gb_out.at[:, lanes_of(chunk)], store_sem.at[1 + chunk]
        )

    store_a().start()

    def end_a(step, carry):
        at = pl.ds(pl.multiple_of(step * LANES, LANES), LANES)
        block = ga[at, :]
        normed = a_high[at, :].astype(jnp.float32) + a_low[at, :].astype(jnp.float32)
        return carry[0] + folded(block), carry[1] + folded(block * normed)

    first, second = lax.fori_loop(0, rows // LANES, end_a, (zero, zero))
    sums[1, 0] = zero
    sums[1, 0, 0:1, :] = jnp.sum(first, axis=0, keepdims=True)
    sums[1, 0, 1:2, :] = jnp.sum(second, axis=0, keepdims=True)
    for chunk in range(chunks):
        mean = stats[chunk, 0:1, :]
        inverse = stats[chunk, 1:2, :]

        def end_b(part, carry):
            home_copy(chunk, part).wait_recv()
            at = pl.ds(pl.multiple_of(part * part_rows, part_rows), part_rows)
            block = raw[chunk, at, :] + swap_in[chunk, at, :]
            raw[chunk, at, :] = block
            normed = (own_raw[chunk, at, :] - mean) * inverse
            return carry[0] + folded(block), carry[1] + folded(block * normed)

        small = jnp.zeros((SUBLANES, LANES), jnp.float32)
        first, second = lax.fori_loop(0, PARTS, end_b, (small, small))
        store_b(chunk).start()
        at = pl.ds(chunk * LANES, LANES)
        sums[1, 0, 2:3, at] = jnp.sum(first, axis=0, keepdims=True)
        sums[1, 0, 3:4, at] = jnp.sum(second, axis=0, keepdims=True)
    ends_out[...] = all_sums(1, lambda b: None)

    stat_near().wait_send()
    stat_ahead().wait_send()

    def drain(chunk, carry):
        for half in range(HALVES):
            swap_copy(chunk, half).wait_send()
        for part in range(PARTS):
            back_copy(chunk, part).wait_send()
            home_copy(chunk, part).wait_send()
        store_b(chunk).wait()
        return carry

    lax.fori_loop(0, chunks, drain, 0)
    store_a().wait()


def per_device(view_a, view_b):
    rows, width = view_a.shape
    row_devices = lax.axis_size("row")
    groups = lax.axis_size("grp")
    batch = rows * row_devices
    bits = row_devices.bit_length() - 1
    chunks = width // LANES
    jobs = chunks // 2 + chunks
    slots = bits + 1
    pair = 2 * LANES
    f32, bf16 = jnp.float32, jnp.bfloat16
    dma = pltpu.SemaphoreType.DMA
    large = jax.ShapeDtypeStruct((rows, width), f32)
    small = jax.ShapeDtypeStruct((SUBLANES, width), f32)
    anywhere = pl.BlockSpec(memory_space=pl.ANY)
    vmem = pl.BlockSpec(memory_space=pltpu.VMEM)
    grad_a, grad_b, totals, ends = pl.pallas_call(
        functools.partial(kernel, groups, row_devices),
        out_shape=[large, large, small, small],
        in_specs=[anywhere, anywhere],
        out_specs=[anywhere, anywhere, vmem, vmem],
        scratch_shapes=[
            pltpu.VMEM((rows, width), bf16),
            pltpu.VMEM((rows, width), bf16),
            pltpu.VMEM((width, rows), bf16),
            pltpu.VMEM((width, rows), bf16),
            pltpu.VMEM((3 * chunks, rows, LANES), f32),
            pltpu.VMEM((chunks, rows, LANES), f32),
            pltpu.VMEM((rows, width), f32),
            pltpu.VMEM((chunks, rows, LANES), f32),
            pltpu.VMEM((chunks, rows, LANES), f32),
            pltpu.VMEM((slots, width, pair), f32),
            pltpu.VMEM((2, width // 2, pair), f32),
            pltpu.VMEM((width // 2, pair), f32),
            [pltpu.VMEM((slots, width >> (b + 1), pair), f32) for b in range(bits)],
            pltpu.VMEM((rows, pair), bf16),
            pltpu.VMEM((rows, pair), bf16),
            pltpu.VMEM((width, pair), bf16),
            pltpu.VMEM((width, pair), bf16),
            pltpu.VMEM((3 * chunks, SUBLANES, LANES), f32),
            pltpu.VMEM((2, bits + 1, SUBLANES, width), f32),
            pltpu.VMEM((2, bits, SUBLANES, width), f32),
            dma((chunks, HALVES)),
            dma((chunks, HALVES)),
            dma((chunks, HALVES)),
            dma((chunks, HALVES)),
            dma((chunks, PARTS)),
            dma((chunks, PARTS)),
            dma((chunks, PARTS)),
            dma((chunks, PARTS)),
            dma((bits, jobs)),
            dma((bits, jobs)),
            dma((bits, jobs)),
            dma((bits, jobs)),
            dma((4,)),
            dma((2, bits)),
            dma((2, bits)),
            dma((1 + chunks,)),
            dma((1 + chunks,)),
        ],
        compiler_params=pltpu.CompilerParams(
            collective_id=0, has_side_effects=True, vmem_limit_bytes=66_000_000
        ),
        name="twins",
    )(view_a, view_b)

    def finish(grad, view, total, square, end, cross):
        mean = total / batch
        scale = jnp.sqrt(square / batch - mean * mean + epsilon)
        normed = (view - mean) / scale
        return (grad - end / batch - normed * (cross / batch)) / scale

    return (
        finish(grad_a, view_a, totals[0], totals[1], ends[0], ends[1]),
        finish(grad_b, view_b, totals[2], totals[3], ends[2], ends[3]),
    )


def solution(mesh):
    placed = (P("row", "grp"), P("row", "grp"))
    return jax.shard_map(
        per_device, mesh=mesh, in_specs=placed, out_specs=placed, check_vma=False
    )
```

```python
import functools

import jax
import jax.numpy as jnp
from jax import lax
from jax.experimental import pallas as pl
from jax.experimental.pallas import tpu as pltpu
from jax.sharding import PartitionSpec as P

epsilon = 1e-05
off_weight = 0.0051
LANES = 128
SUBLANES = 8
HALVES = 1
PARTS = 4
BLOCK = 256
WINDOW = 1
HOLD = 2
MESH = pl.DeviceIdType.MESH


def split(block):
    high = block.astype(jnp.bfloat16)
    return high, (block - high.astype(jnp.float32)).astype(jnp.bfloat16)


def dot3(left_high, left_low, right_high, right_low, contract):
    def one(left, right):
        return lax.dot_general(
            left, right, (contract, ((), ())), preferred_element_type=jnp.float32
        )

    cross = one(left_high, right_low) + one(left_low, right_high)
    return cross + one(left_high, right_high)


def kernel(
    groups,
    row_devices,
    view_a,
    view_b,
    ga_out,
    gb_out,
    totals_out,
    ends_out,
    a_high,
    a_low,
    at_high,
    at_low,
    raw,
    own_raw,
    ga,
    back_in,
    swap_in,
    pen,
    share_send,
    share_kept,
    share_in,
    block_high,
    block_low,
    pen_high,
    pen_low,
    stats,
    sums,
    sums_in,
    swap_send_sem,
    swap_recv_sem,
    hop_send_sem,
    hop_recv_sem,
    back_send_sem,
    back_recv_sem,
    home_send_sem,
    home_recv_sem,
    share_send_sem,
    share_recv_sem,
    pen_send_sem,
    pen_recv_sem,
    stat_sem,
    sums_send_sem,
    sums_recv_sem,
    load_sem,
    store_sem,
):
    rows, width = a_high.shape
    chunks = width // LANES
    own_jobs = chunks // 2
    jobs = own_jobs + chunks
    bits = row_devices.bit_length() - 1
    slots = 2 * bits
    delay = 2 * bits - 1
    hold = max(chunks - HOLD, delay + 1)
    batch = rows * row_devices
    pair = 2 * LANES
    half_rows = rows // HALVES
    part_rows = rows // PARTS

    group = lax.axis_index("grp")
    row = lax.axis_index("row")
    sign = 1 - 2 * lax.rem(group, 2)
    near = (group + sign, row)
    ahead = (lax.rem(group + groups + 2 * sign, groups), row)
    behind = (lax.rem(group + groups - 2 * sign, groups), row)
    digit = [lax.rem(lax.div(row, 1 << b), 2) for b in range(bits)]
    peer = [(group, row + (1 - 2 * digit[b]) * (1 << b)) for b in range(bits)]
    size = [width >> (b + 1) for b in range(bits)]
    start = [0]
    for b in range(bits):
        start.append(start[b] + digit[b] * size[b])
    away = [start[b] + (1 - digit[b]) * size[b] for b in range(bits)]
    share = size[-1]

    barrier = pltpu.get_barrier_semaphore()
    for device in [near, ahead, behind] + peer:
        pl.semaphore_signal(barrier, inc=1, device_id=device, device_id_type=MESH)
    pl.semaphore_wait(barrier, 3 + bits)

    def remote(source, target, send, recv, device):
        return pltpu.make_async_remote_copy(
            src_ref=source,
            dst_ref=target,
            send_sem=send,
            recv_sem=recv,
            device_id=device,
            device_id_type=MESH,
        )

    def lanes_of(chunk):
        return pl.ds(pl.multiple_of(chunk * LANES, LANES), LANES)

    def swap_copy(chunk, half):
        at = pl.ds(half * half_rows, half_rows)
        return remote(
            view_b.at[at, lanes_of(chunk)],
            raw.at[chunks + chunk, at, :],
            swap_send_sem.at[chunk, half],
            swap_recv_sem.at[chunk, half],
            near,
        )

    def hop_copy(chunk, half):
        at = pl.ds(half * half_rows, half_rows)
        return remote(
            raw.at[chunks + chunk, at, :],
            raw.at[2 * chunks + chunk, at, :],
            hop_send_sem.at[chunk, half],
            hop_recv_sem.at[chunk, half],
            ahead,
        )

    def back_copy(chunk, part):
        at = pl.ds(pl.multiple_of(part * part_rows, part_rows), part_rows)
        return remote(
            raw.at[2 * chunks + chunk, at, :],
            back_in.at[chunk, at, :],
            back_send_sem.at[chunk, part],
            back_recv_sem.at[chunk, part],
            behind,
        )

    def home_copy(chunk, part):
        at = pl.ds(pl.multiple_of(part * part_rows, part_rows), part_rows)
        return remote(
            raw.at[chunks + chunk, at, :],
            swap_in.at[chunk, at, :],
            home_send_sem.at[chunk, part],
            home_recv_sem.at[chunk, part],
            near,
        )

    def share_copy(job, b):
        if b == 0:
            source = share_send.at[lax.rem(job, 2)]
        else:
            at = pl.ds(pl.multiple_of(away[b] - start[b], size[b]), size[b])
            source = share_in[b - 1].at[lax.rem(job, slots), at, :]
        return remote(
            source,
            share_in[b].at[lax.rem(job, slots)],
            share_send_sem.at[b, job],
            share_recv_sem.at[b, job],
            peer[b],
        )

    def pen_copy(job, b):
        at = pl.ds(pl.multiple_of(start[b + 1], size[b]), size[b])
        return remote(
            pen.at[lax.rem(job, slots), at, :],
            pen.at[lax.rem(job, slots), at, :],
            pen_send_sem.at[b, job],
            pen_recv_sem.at[b, job],
            peer[b],
        )

    def sums_copy(which, b):
        return remote(
            sums.at[which, b],
            sums_in.at[which, b],
            sums_send_sem.at[which, b],
            sums_recv_sem.at[which, b],
            peer[b],
        )

    def all_sums(which, between):
        for b in range(bits):
            sums_copy(which, b).start()
            between(b)
            sums_copy(which, b).wait()
            sums[which, b + 1] = sums[which, b] + sums_in[which, b]
        return sums[which, bits]

    def stat_near():
        return remote(
            stats.at[pl.ds(0, chunks)],
            stats.at[pl.ds(chunks, chunks)],
            stat_sem.at[0],
            stat_sem.at[1],
            near,
        )

    def stat_ahead():
        return remote(
            stats.at[pl.ds(chunks, chunks)],
            stats.at[pl.ds(2 * chunks, chunks)],
            stat_sem.at[2],
            stat_sem.at[3],
            ahead,
        )

    for chunk in range(min(WINDOW, chunks)):
        for half in range(HALVES):
            swap_copy(chunk, half).start()
    load_a = pltpu.make_async_copy(view_a, ga, load_sem.at[0])
    load_a.start()

    def load_own(chunk):
        return pltpu.make_async_copy(
            view_b.at[:, lanes_of(chunk)], own_raw.at[chunk], load_sem.at[1 + chunk]
        )

    for chunk in range(chunks):
        load_own(chunk).start()
    load_a.wait()

    def folded(block):
        return jnp.sum(block.reshape(-1, SUBLANES, block.shape[-1]), axis=0)

    def add_a(step, carry):
        at = pl.ds(pl.multiple_of(step * LANES, LANES), LANES)
        block = ga[at, :]
        return carry[0] + folded(block), carry[1] + folded(block * block)

    zero = jnp.zeros((SUBLANES, width), jnp.float32)
    def relay(chunk, half):
        swap_copy(chunk, half).wait_recv()
        hop_copy(chunk, half).start()

        @pl.when(chunk + WINDOW < chunks)
        def _():
            swap_copy(chunk + WINDOW, half).start()

    first, second = lax.fori_loop(0, rows // LANES, add_a, (zero, zero))
    sums[0, 0] = zero
    sums[0, 0, 0:1, :] = jnp.sum(first, axis=0, keepdims=True)
    sums[0, 0, 1:2, :] = jnp.sum(second, axis=0, keepdims=True)
    for chunk in range(chunks):
        load_own(chunk).wait()
        block = own_raw[chunk]
        raw[chunk] = block
        at = pl.ds(chunk * LANES, LANES)
        sums[0, 0, 2:3, at] = jnp.sum(folded(block), axis=0, keepdims=True)
        sums[0, 0, 3:4, at] = jnp.sum(folded(block * block), axis=0, keepdims=True)

    totals = all_sums(0, lambda b: None)
    relay(0, 0)
    totals_out[...] = totals

    def mean_and_inverse(total, square):
        mean = total / batch
        scale = jnp.sqrt(square / batch - mean * mean + epsilon)
        return mean, 1.0 / scale

    mean_a, inverse_a = mean_and_inverse(totals[0:1, :], totals[1:2, :])
    mean_b, inverse_b = mean_and_inverse(totals[2:3, :], totals[3:4, :])
    for chunk in range(chunks):
        at = slice(chunk * LANES, (chunk + 1) * LANES)
        stats[chunk] = jnp.zeros((SUBLANES, LANES), jnp.float32)
        stats[chunk, 0:1, :] = mean_b[:, at]
        stats[chunk, 1:2, :] = inverse_b[:, at]
    stat_near().start()

    def norm_a(step, carry):
        at = pl.ds(pl.multiple_of(step * LANES, LANES), LANES)
        block = (ga[at, :] - mean_a) * inverse_a
        a_high[at, :], a_low[at, :] = split(block)
        at_high[:, at], at_low[:, at] = split(block.T)
        ga[at, :] = jnp.zeros_like(block)
        return carry

    lax.fori_loop(0, rows // LANES // 2, norm_a, 0)
    lax.fori_loop(rows // LANES // 2, rows // LANES, norm_a, 0)
    stat_near().wait_recv()
    stat_ahead().start()
    def own_of(job):
        return job >= chunks, job - chunks

    def places(job):
        is_own, index = own_of(job)
        chunk = job
        first = jnp.where(is_own, 2 * index, chunks + chunk)
        second = jnp.where(is_own, 2 * index + 1, 2 * chunks + chunk)
        return first, second

    def when_pair(job, action):
        pl.when(job < chunks)(lambda: action(job))

    def load_block(job):
        for part, place in enumerate(places(job)):
            mean = stats[place, 0:1, :]
            inverse = stats[place, 1:2, :]
            high, low = split((raw[place] - mean) * inverse)
            at = slice(part * LANES, (part + 1) * LANES)
            block_high[:, at] = high
            block_low[:, at] = low

    def correlate(job):
        @pl.when(job == 0)
        def _():
            stat_ahead().wait_recv()

        def arrived(chunk):
            for half in range(HALVES):
                hop_copy(chunk, half).wait_recv()

        when_pair(job, arrived)
        load_block(job)

        def part_of(target, base):
            count = min(BLOCK, size[0])

            def body(step, carry):
                offset = pl.multiple_of(step * count, count)
                at = pl.ds(pl.multiple_of(base + offset, count), count)
                target[pl.ds(offset, count), :] = dot3(
                    at_high[at, :],
                    at_low[at, :],
                    block_high[...],
                    block_low[...],
                    ((1,), (0,)),
                ) * (1.0 / batch)
                return carry

            lax.fori_loop(0, size[0] // count, body, 0)

        part_of(share_send.at[lax.rem(job, 2)], away[0])
        share_copy(job, 0).start()
        part_of(share_kept, start[1])

    def reduce_step(job, b):
        share_copy(job, b).wait()
        slot = lax.rem(job, slots)
        if b == 0:
            kept = share_kept[...]
        else:
            at = pl.ds(pl.multiple_of(start[b + 1] - start[b], size[b]), size[b])
            kept = share_in[b - 1][slot, at, :]
        total = kept + share_in[b][slot]
        if b < bits - 1:
            share_in[b][slot] = total
            share_copy(job, b + 1).start()
            return
        shape = (share, pair)
        row_index = start[bits] + lax.broadcasted_iota(jnp.int32, shape, 0)
        is_own, index = own_of(job)
        base = jnp.where(is_own, index * pair, -width)
        column = base + lax.broadcasted_iota(jnp.int32, shape, 1)
        value = jnp.where(
            column == row_index, -2.0 * (1.0 - total), 2.0 * off_weight * total
        )
        at = pl.ds(pl.multiple_of(start[bits], share), share)
        pen[slot, at, :] = value
        pen_copy(job, bits - 1).start()

    def gather_step(job, b):
        pen_copy(job, b).wait()
        pen_copy(job, b - 1).start()

    def consume(job):
        pen_copy(job, 0).wait()
        slot = lax.rem(job, slots)
        pen_high[...], pen_low[...] = split(pen[slot])
        load_block(job)
        first, second = places(job)

        def hopped(chunk):
            for half in range(HALVES):
                hop_copy(chunk, half).wait_send()

        when_pair(job, hopped)

        def contribute(step, carry):
            at = pl.ds(pl.multiple_of(step * BLOCK, BLOCK), BLOCK)
            value = dot3(
                a_high[at, :], a_low[at, :], pen_high[...], pen_low[...], ((1,), (0,))
            )
            raw[first, at, :] = value[:, :LANES]
            raw[second, at, :] = value[:, LANES:]
            return carry

        lax.fori_loop(0, rows // BLOCK, contribute, 0)

        def accumulate(step, carry):
            at = pl.ds(pl.multiple_of(step * BLOCK, BLOCK), BLOCK)
            ga[at, :] += dot3(
                block_high[at, :],
                block_low[at, :],
                pen_high[...],
                pen_low[...],
                ((1,), (1,)),
            )
            return carry

        lax.fori_loop(0, rows // BLOCK, accumulate, 0)

    def step_of(job, k):
        if k <= bits:
            reduce_step(job, k - 1)
        else:
            gather_step(job, 2 * bits - k)

    def send_home(chunk):
        def body(part, carry):
            back_copy(chunk, part).wait_recv()
            at = pl.ds(pl.multiple_of(part * part_rows, part_rows), part_rows)
            raw[chunks + chunk, at, :] += back_in[chunk, at, :]
            home_copy(chunk, part).start()
            return carry

        lax.fori_loop(0, PARTS, body, 0)

    def tick(t, carry):
        following = t + 1
        relays = following < chunks

        @pl.when(relays)
        def _():
            relay(following, 0)

        def run(job, action):
            pl.when(jnp.logical_and(job >= 0, job < jobs))(lambda: action(job))

        def send_back(chunk):
            for part in range(PARTS):
                back_copy(chunk, part).start()

        turn = t - hold
        pl.when(jnp.logical_and(turn >= 0, turn < chunks))(lambda: send_back(turn))
        home = turn - 1
        pl.when(jnp.logical_and(home >= 0, home < chunks))(lambda: send_home(home))
        run(t, correlate)
        run(t - delay, consume)
        for k in range(delay, 0, -1):
            run(t - k + 1, functools.partial(step_of, k=k))
        return carry

    lax.fori_loop(0, max(jobs + delay, hold + chunks + 1), tick, 0)

    def store_a():
        return pltpu.make_async_copy(ga, ga_out, store_sem.at[0])

    def store_b(chunk):
        return pltpu.make_async_copy(
            raw.at[chunk], gb_out.at[:, lanes_of(chunk)], store_sem.at[1 + chunk]
        )

    store_a().start()

    def end_a(step, carry):
        at = pl.ds(pl.multiple_of(step * LANES, LANES), LANES)
        block = ga[at, :]
        normed = a_high[at, :].astype(jnp.float32) + a_low[at, :].astype(jnp.float32)
        return carry[0] + folded(block), carry[1] + folded(block * normed)

    first, second = lax.fori_loop(0, rows // LANES, end_a, (zero, zero))
    sums[1, 0] = zero
    sums[1, 0, 0:1, :] = jnp.sum(first, axis=0, keepdims=True)
    sums[1, 0, 1:2, :] = jnp.sum(second, axis=0, keepdims=True)
    for chunk in range(chunks):
        mean = stats[chunk, 0:1, :]
        inverse = stats[chunk, 1:2, :]

        def end_b(part, carry):
            home_copy(chunk, part).wait_recv()
            at = pl.ds(pl.multiple_of(part * part_rows, part_rows), part_rows)
            block = raw[chunk, at, :] + swap_in[chunk, at, :]
            raw[chunk, at, :] = block
            normed = (own_raw[chunk, at, :] - mean) * inverse
            return carry[0] + folded(block), carry[1] + folded(block * normed)

        small = jnp.zeros((SUBLANES, LANES), jnp.float32)
        first, second = lax.fori_loop(0, PARTS, end_b, (small, small))
        store_b(chunk).start()
        at = pl.ds(chunk * LANES, LANES)
        sums[1, 0, 2:3, at] = jnp.sum(first, axis=0, keepdims=True)
        sums[1, 0, 3:4, at] = jnp.sum(second, axis=0, keepdims=True)
    ends_out[...] = all_sums(1, lambda b: None)

    stat_near().wait_send()
    stat_ahead().wait_send()

    def drain(chunk, carry):
        for half in range(HALVES):
            swap_copy(chunk, half).wait_send()
        for part in range(PARTS):
            back_copy(chunk, part).wait_send()
            home_copy(chunk, part).wait_send()
        store_b(chunk).wait()
        return carry

    lax.fori_loop(0, chunks, drain, 0)
    store_a().wait()


def per_device(view_a, view_b):
    rows, width = view_a.shape
    row_devices = lax.axis_size("row")
    groups = lax.axis_size("grp")
    batch = rows * row_devices
    bits = row_devices.bit_length() - 1
    chunks = width // LANES
    jobs = chunks // 2 + chunks
    slots = 2 * bits
    pair = 2 * LANES
    f32, bf16 = jnp.float32, jnp.bfloat16
    dma = pltpu.SemaphoreType.DMA
    large = jax.ShapeDtypeStruct((rows, width), f32)
    small = jax.ShapeDtypeStruct((SUBLANES, width), f32)
    anywhere = pl.BlockSpec(memory_space=pl.ANY)
    vmem = pl.BlockSpec(memory_space=pltpu.VMEM)
    grad_a, grad_b, totals, ends = pl.pallas_call(
        functools.partial(kernel, groups, row_devices),
        out_shape=[large, large, small, small],
        in_specs=[anywhere, anywhere],
        out_specs=[anywhere, anywhere, vmem, vmem],
        scratch_shapes=[
            pltpu.VMEM((rows, width), bf16),
            pltpu.VMEM((rows, width), bf16),
            pltpu.VMEM((width, rows), bf16),
            pltpu.VMEM((width, rows), bf16),
            pltpu.VMEM((3 * chunks, rows, LANES), f32),
            pltpu.VMEM((chunks, rows, LANES), f32),
            pltpu.VMEM((rows, width), f32),
            pltpu.VMEM((chunks, rows, LANES), f32),
            pltpu.VMEM((chunks, rows, LANES), f32),
            pltpu.VMEM((slots, width, pair), f32),
            pltpu.VMEM((2, width // 2, pair), f32),
            pltpu.VMEM((width // 2, pair), f32),
            [pltpu.VMEM((slots, width >> (b + 1), pair), f32) for b in range(bits)],
            pltpu.VMEM((rows, pair), bf16),
            pltpu.VMEM((rows, pair), bf16),
            pltpu.VMEM((width, pair), bf16),
            pltpu.VMEM((width, pair), bf16),
            pltpu.VMEM((3 * chunks, SUBLANES, LANES), f32),
            pltpu.VMEM((2, bits + 1, SUBLANES, width), f32),
            pltpu.VMEM((2, bits, SUBLANES, width), f32),
            dma((chunks, HALVES)),
            dma((chunks, HALVES)),
            dma((chunks, HALVES)),
            dma((chunks, HALVES)),
            dma((chunks, PARTS)),
            dma((chunks, PARTS)),
            dma((chunks, PARTS)),
            dma((chunks, PARTS)),
            dma((bits, jobs)),
            dma((bits, jobs)),
            dma((bits, jobs)),
            dma((bits, jobs)),
            dma((4,)),
            dma((2, bits)),
            dma((2, bits)),
            dma((1 + chunks,)),
            dma((1 + chunks,)),
        ],
        compiler_params=pltpu.CompilerParams(
            collective_id=0, has_side_effects=True, vmem_limit_bytes=66_000_000
        ),
        name="twins",
    )(view_a, view_b)

    def finish(grad, view, total, square, end, cross):
        mean = total / batch
        scale = jnp.sqrt(square / batch - mean * mean + epsilon)
        normed = (view - mean) / scale
        return (grad - end / batch - normed * (cross / batch)) / scale

    return (
        finish(grad_a, view_a, totals[0], totals[1], ends[0], ends[1]),
        finish(grad_b, view_b, totals[2], totals[3], ends[2], ends[3]),
    )


def solution(mesh):
    placed = (P("row", "grp"), P("row", "grp"))
    return jax.shard_map(
        per_device, mesh=mesh, in_specs=placed, out_specs=placed, check_vma=False
    )
```

```python
import functools

import jax
import jax.numpy as jnp
from jax import lax
from jax.experimental import pallas as pl
from jax.experimental.pallas import tpu as pltpu
from jax.sharding import PartitionSpec as P

epsilon = 1e-05
off_weight = 0.0051
LANES = 128
SUBLANES = 8
HALVES = 1
PARTS = 2
BLOCK = 256
VMEM_LIMIT = 50 << 20
HOLD = 2
WINDOW = 1
BACK_AT = 2
HOME_AT = 3
MESH = pl.DeviceIdType.MESH


def split(block):
    high = block.astype(jnp.bfloat16)
    return high, (block - high.astype(jnp.float32)).astype(jnp.bfloat16)


def dot3(left_high, left_low, right_high, right_low, contract):
    def one(left, right):
        return lax.dot_general(
            left, right, (contract, ((), ())), preferred_element_type=jnp.float32
        )

    cross = one(left_high, right_low) + one(left_low, right_high)
    return cross + one(left_high, right_high)


def kernel(
    groups,
    row_devices,
    view_a,
    view_b,
    ga,
    gb_out,
    a_high,
    a_low,
    at_high,
    at_low,
    raw,
    own_raw,
    back_in,
    swap_in,
    pen,
    share_send,
    share_kept,
    share_in,
    block_high,
    block_low,
    pen_high,
    pen_low,
    stats,
    sums,
    sums_in,
    swap_send_sem,
    swap_recv_sem,
    hop_send_sem,
    hop_recv_sem,
    back_send_sem,
    back_recv_sem,
    home_send_sem,
    home_recv_sem,
    share_send_sem,
    share_recv_sem,
    pen_send_sem,
    pen_recv_sem,
    stat_sem,
    sums_send_sem,
    sums_recv_sem,
    load_sem,
):
    rows, width = a_high.shape
    chunks = width // LANES
    own_jobs = chunks // 2
    jobs = own_jobs + chunks
    bits = row_devices.bit_length() - 1
    slots = 2 * bits
    delay = 2 * bits - 1
    hold = max(chunks - HOLD, delay + 1)
    batch = rows * row_devices
    pair = 2 * LANES
    half_rows = rows // HALVES
    part_rows = rows // PARTS

    group = lax.axis_index("grp")
    row = lax.axis_index("row")
    sign = 1 - 2 * lax.rem(group, 2)
    near = (group + sign, row)
    ahead = (lax.rem(group + groups + 2 * sign, groups), row)
    behind = (lax.rem(group + groups - 2 * sign, groups), row)
    digit = [lax.rem(lax.div(row, 1 << b), 2) for b in range(bits)]
    peer = [(group, row + (1 - 2 * digit[b]) * (1 << b)) for b in range(bits)]
    size = [width >> (b + 1) for b in range(bits)]
    start = [0]
    for b in range(bits):
        start.append(start[b] + digit[b] * size[b])
    away = [start[b] + (1 - digit[b]) * size[b] for b in range(bits)]
    share = size[-1]

    barrier = pltpu.get_barrier_semaphore()
    for device in [near, ahead, behind] + peer:
        pl.semaphore_signal(barrier, inc=1, device_id=device, device_id_type=MESH)
    pl.semaphore_wait(barrier, 3 + bits)

    def remote(source, target, send, recv, device):
        return pltpu.make_async_remote_copy(
            src_ref=source,
            dst_ref=target,
            send_sem=send,
            recv_sem=recv,
            device_id=device,
            device_id_type=MESH,
        )

    def lanes_of(chunk):
        return pl.ds(pl.multiple_of(chunk * LANES, LANES), LANES)

    def swap_copy(chunk, half):
        at = pl.ds(half * half_rows, half_rows)
        return remote(
            view_b.at[at, lanes_of(chunk)],
            raw.at[chunks + chunk, at, :],
            swap_send_sem.at[chunk, half],
            swap_recv_sem.at[chunk, half],
            near,
        )

    def hop_copy(chunk, half):
        at = pl.ds(half * half_rows, half_rows)
        return remote(
            raw.at[chunks + chunk, at, :],
            raw.at[2 * chunks + chunk, at, :],
            hop_send_sem.at[chunk, half],
            hop_recv_sem.at[chunk, half],
            ahead,
        )

    def back_copy(chunk, part):
        at = pl.ds(pl.multiple_of(part * part_rows, part_rows), part_rows)
        return remote(
            raw.at[2 * chunks + chunk, at, :],
            back_in.at[chunk, at, :],
            back_send_sem.at[chunk, part],
            back_recv_sem.at[chunk, part],
            behind,
        )

    def home_copy(chunk, part):
        at = pl.ds(pl.multiple_of(part * part_rows, part_rows), part_rows)
        return remote(
            raw.at[chunks + chunk, at, :],
            swap_in.at[chunk, at, :],
            home_send_sem.at[chunk, part],
            home_recv_sem.at[chunk, part],
            near,
        )

    def share_copy(job, b):
        if b == 0:
            source = share_send.at[lax.rem(job, 2)]
        else:
            at = pl.ds(pl.multiple_of(away[b] - start[b], size[b]), size[b])
            source = share_in[b - 1].at[lax.rem(job, slots), at, :]
        return remote(
            source,
            share_in[b].at[lax.rem(job, slots)],
            share_send_sem.at[b, job],
            share_recv_sem.at[b, job],
            peer[b],
        )

    def pen_copy(job, b):
        at = pl.ds(pl.multiple_of(start[b + 1], size[b]), size[b])
        return remote(
            pen.at[lax.rem(job, slots), at, :],
            pen.at[lax.rem(job, slots), at, :],
            pen_send_sem.at[b, job],
            pen_recv_sem.at[b, job],
            peer[b],
        )

    def sums_copy(which, b):
        return remote(
            sums.at[which, b],
            sums_in.at[which, b],
            sums_send_sem.at[which, b],
            sums_recv_sem.at[which, b],
            peer[b],
        )

    def all_sums(which):
        for b in range(bits):
            sums_copy(which, b).start()
            sums_copy(which, b).wait()
            sums[which, b + 1] = sums[which, b] + sums_in[which, b]
        return sums[which, bits]

    def stat_near():
        return remote(
            stats.at[pl.ds(0, chunks)],
            stats.at[pl.ds(chunks, chunks)],
            stat_sem.at[0],
            stat_sem.at[1],
            near,
        )

    def stat_ahead():
        return remote(
            stats.at[pl.ds(chunks, chunks)],
            stats.at[pl.ds(2 * chunks, chunks)],
            stat_sem.at[2],
            stat_sem.at[3],
            ahead,
        )

    swap_copy(0, 0).start()
    load_a = pltpu.make_async_copy(view_a, ga, load_sem.at[0])
    load_a.start()

    def load_own(chunk):
        return pltpu.make_async_copy(
            view_b.at[:, lanes_of(chunk)], own_raw.at[chunk], load_sem.at[1 + chunk]
        )

    for chunk in range(chunks):
        load_own(chunk).start()
    load_a.wait()
    for half in range(1, HALVES):
        swap_copy(0, half).start()

    def folded(block):
        return jnp.sum(block.reshape(-1, SUBLANES, block.shape[-1]), axis=0)

    def add_a(step, carry):
        at = pl.ds(pl.multiple_of(step * LANES, LANES), LANES)
        block = ga[at, :]
        return carry[0] + folded(block), carry[1] + folded(block * block)

    zero = jnp.zeros((SUBLANES, width), jnp.float32)
    def relay(chunk, half):
        swap_copy(chunk, half).wait_recv()
        hop_copy(chunk, half).start()

        @pl.when(chunk + WINDOW < chunks)
        def _():
            swap_copy(chunk + WINDOW, half).start()

    first, second = lax.fori_loop(0, rows // LANES, add_a, (zero, zero))
    sums[0, 0] = zero
    sums[0, 0, 0:1, :] = jnp.sum(first, axis=0, keepdims=True)
    sums[0, 0, 1:2, :] = jnp.sum(second, axis=0, keepdims=True)
    for chunk in range(chunks):
        load_own(chunk).wait()
        block = own_raw[chunk]
        raw[chunk] = block
        at = pl.ds(chunk * LANES, LANES)
        sums[0, 0, 2:3, at] = jnp.sum(folded(block), axis=0, keepdims=True)
        sums[0, 0, 3:4, at] = jnp.sum(folded(block * block), axis=0, keepdims=True)

    for chunk in range(1, WINDOW):
        for half in range(HALVES):
            swap_copy(chunk, half).start()
    relay(0, 0)
    totals = all_sums(0)
    for half in range(1, HALVES):
        relay(0, half)

    def mean_and_inverse(total, square):
        mean = total / batch
        scale = jnp.sqrt(square / batch - mean * mean + epsilon)
        return mean, 1.0 / scale

    mean_a, inverse_a = mean_and_inverse(totals[0:1, :], totals[1:2, :])
    mean_b, inverse_b = mean_and_inverse(totals[2:3, :], totals[3:4, :])
    for chunk in range(chunks):
        at = slice(chunk * LANES, (chunk + 1) * LANES)
        stats[chunk] = jnp.zeros((SUBLANES, LANES), jnp.float32)
        stats[chunk, 0:1, :] = mean_b[:, at]
        stats[chunk, 1:2, :] = inverse_b[:, at]
    stat_near().start()

    def norm_a(step, carry):
        at = pl.ds(pl.multiple_of(step * LANES, LANES), LANES)
        block = (ga[at, :] - mean_a) * inverse_a
        a_high[at, :], a_low[at, :] = split(block)
        at_high[:, at], at_low[:, at] = split(block.T)
        ga[at, :] = jnp.zeros_like(block)
        return carry

    lax.fori_loop(0, rows // LANES // 2, norm_a, 0)
    lax.fori_loop(rows // LANES // 2, rows // LANES, norm_a, 0)
    stat_near().wait_recv()
    stat_ahead().start()
    def own_of(job):
        return job >= chunks, job - chunks

    def places(job):
        is_own, index = own_of(job)
        chunk = job
        first = jnp.where(is_own, 2 * index, chunks + chunk)
        second = jnp.where(is_own, 2 * index + 1, 2 * chunks + chunk)
        return first, second

    def when_pair(job, action):
        pl.when(job < chunks)(lambda: action(job))

    def load_block(job):
        for part, place in enumerate(places(job)):
            mean = stats[place, 0:1, :]
            inverse = stats[place, 1:2, :]
            high, low = split((raw[place] - mean) * inverse)
            at = slice(part * LANES, (part + 1) * LANES)
            block_high[:, at] = high
            block_low[:, at] = low

    def correlate(job):
        @pl.when(job == 0)
        def _():
            stat_ahead().wait_recv()

        def arrived(chunk):
            for half in range(HALVES):
                hop_copy(chunk, half).wait_recv()

        when_pair(job, arrived)
        load_block(job)

        def part_of(target, base):
            count = min(BLOCK, size[0])

            def body(step, carry):
                offset = pl.multiple_of(step * count, count)
                at = pl.ds(pl.multiple_of(base + offset, count), count)
                target[pl.ds(offset, count), :] = dot3(
                    at_high[at, :],
                    at_low[at, :],
                    block_high[...],
                    block_low[...],
                    ((1,), (0,)),
                ) * (1.0 / batch)
                return carry

            lax.fori_loop(0, size[0] // count, body, 0)

        part_of(share_send.at[lax.rem(job, 2)], away[0])
        share_copy(job, 0).start()
        part_of(share_kept, start[1])

    def reduce_step(job, b):
        share_copy(job, b).wait()
        slot = lax.rem(job, slots)
        if b == 0:
            kept = share_kept[...]
        else:
            at = pl.ds(pl.multiple_of(start[b + 1] - start[b], size[b]), size[b])
            kept = share_in[b - 1][slot, at, :]
        total = kept + share_in[b][slot]
        if b < bits - 1:
            share_in[b][slot] = total
            share_copy(job, b + 1).start()
            return
        shape = (share, pair)
        row_index = start[bits] + lax.broadcasted_iota(jnp.int32, shape, 0)
        is_own, index = own_of(job)
        base = jnp.where(is_own, index * pair, -width)
        column = base + lax.broadcasted_iota(jnp.int32, shape, 1)
        value = jnp.where(
            column == row_index, -2.0 * (1.0 - total), 2.0 * off_weight * total
        )
        at = pl.ds(pl.multiple_of(start[bits], share), share)
        pen[slot, at, :] = value
        pen_copy(job, bits - 1).start()

    def gather_step(job, b):
        pen_copy(job, b).wait()
        pen_copy(job, b - 1).start()

    def consume(job):
        pen_copy(job, 0).wait()
        slot = lax.rem(job, slots)
        pen_high[...], pen_low[...] = split(pen[slot])
        load_block(job)
        first, second = places(job)

        def hopped(chunk):
            for half in range(HALVES):
                hop_copy(chunk, half).wait_send()

        when_pair(job, hopped)

        def contribute(step, carry):
            at = pl.ds(pl.multiple_of(step * BLOCK, BLOCK), BLOCK)
            value = dot3(
                a_high[at, :], a_low[at, :], pen_high[...], pen_low[...], ((1,), (0,))
            )
            raw[first, at, :] = value[:, :LANES]
            raw[second, at, :] = value[:, LANES:]
            return carry

        lax.fori_loop(0, rows // BLOCK, contribute, 0)

        def accumulate(step, carry):
            at = pl.ds(pl.multiple_of(step * BLOCK, BLOCK), BLOCK)
            ga[at, :] += dot3(
                block_high[at, :],
                block_low[at, :],
                pen_high[...],
                pen_low[...],
                ((1,), (1,)),
            )
            return carry

        lax.fori_loop(0, rows // BLOCK, accumulate, 0)

    def step_of(job, k):
        if k <= bits:
            reduce_step(job, k - 1)
        else:
            gather_step(job, 2 * bits - k)

    def send_home(chunk):
        def body(part, carry):
            back_copy(chunk, part).wait_recv()
            at = pl.ds(pl.multiple_of(part * part_rows, part_rows), part_rows)
            raw[chunks + chunk, at, :] += back_in[chunk, at, :]
            home_copy(chunk, part).start()
            return carry

        lax.fori_loop(0, PARTS, body, 0)

    def tick(t, carry):
        following = t + 1
        relays = following < chunks

        @pl.when(relays)
        def _():
            relay(following, 0)

        def run(job, action):
            pl.when(jnp.logical_and(job >= 0, job < jobs))(lambda: action(job))

        turn = t - hold

        def send_back(first, last):
            for part in range(first, last):
                back_copy(turn, part).start()

        inside = jnp.logical_and(turn >= 0, turn < chunks)
        home = turn - 1
        sent = jnp.logical_and(home >= 0, home < chunks - 1)

        def backs(place):
            if place == BACK_AT:
                pl.when(inside)(lambda: send_back(0, PARTS))

        def homes(place):
            if place == HOME_AT:
                pl.when(sent)(lambda: send_home(home))

        backs(0)
        homes(0)
        run(t, correlate)
        backs(1)
        homes(1)

        @pl.when(relays)
        def _():
            for half in range(1, HALVES):
                relay(following, half)

        run(t - delay, consume)
        backs(2)
        homes(2)
        for k in range(delay, 0, -1):
            run(t - k + 1, functools.partial(step_of, k=k))
        backs(3)
        homes(3)
        return carry

    lax.fori_loop(0, max(jobs + delay, hold + chunks), tick, 0)

    def end_a(step, carry):
        at = pl.ds(pl.multiple_of(step * LANES, LANES), LANES)
        block = ga[at, :]
        return carry[0] + folded(block), carry[1] + folded(block * normed_a(at))

    def normed_a(at):
        return a_high[at, :].astype(jnp.float32) + a_low[at, :].astype(jnp.float32)

    first, second = lax.fori_loop(0, rows // LANES, end_a, (zero, zero))
    sums[1, 0] = zero
    sums[1, 0, 0:1, :] = jnp.sum(first, axis=0, keepdims=True)
    sums[1, 0, 1:2, :] = jnp.sum(second, axis=0, keepdims=True)
    sums_copy(1, 0).start()
    sums[2, 0] = zero

    def normed_b(chunk, at):
        mean = stats[chunk, 0:1, :]
        return (own_raw[chunk, at, :] - mean) * stats[chunk, 1:2, :]

    def end_b(chunk):
        def body(part, carry):
            home_copy(chunk, part).wait_recv()
            at = pl.ds(pl.multiple_of(part * part_rows, part_rows), part_rows)
            block = raw[chunk, at, :] + swap_in[chunk, at, :]
            raw[chunk, at, :] = block
            cross = folded(block * normed_b(chunk, at))
            return carry[0] + folded(block), carry[1] + cross

        small = jnp.zeros((SUBLANES, LANES), jnp.float32)
        first, second = lax.fori_loop(0, PARTS, body, (small, small))
        at = pl.ds(chunk * LANES, LANES)
        sums[2, 0, 0:1, at] = jnp.sum(first, axis=0, keepdims=True)
        sums[2, 0, 1:2, at] = jnp.sum(second, axis=0, keepdims=True)

    for chunk in range(chunks - 2):
        end_b(chunk)
    send_home(chunks - 1)
    for b in range(bits):
        if b > 0:
            sums_copy(1, b).start()
        sums_copy(1, b).wait()
        sums[1, b + 1] = sums[1, b] + sums_in[1, b]
    ends = sums[1, bits] / batch
    end_mean, end_cross = ends[0:1, :], ends[1:2, :]

    def finish_a(step, carry):
        at = pl.ds(pl.multiple_of(step * LANES, LANES), LANES)
        ga[at, :] = (ga[at, :] - end_mean - normed_a(at) * end_cross) * inverse_a
        return carry

    lax.fori_loop(0, rows // LANES, finish_a, 0)
    for chunk in range(chunks - 2, chunks):
        end_b(chunk)
    for b in range(bits):
        sums_copy(2, b).start()
        sums_copy(2, b).wait()
        sums[2, b + 1] = sums[2, b] + sums_in[2, b]
    for chunk in range(chunks):
        at = pl.ds(chunk * LANES, LANES)
        end_mean = sums[2, bits, 0:1, at] / batch
        end_cross = sums[2, bits, 1:2, at] / batch
        inverse = stats[chunk, 1:2, :]

        def finish_b(part, carry):
            here = pl.ds(pl.multiple_of(part * part_rows, part_rows), part_rows)
            removed = end_mean + normed_b(chunk, here) * end_cross
            gb_out[here, at] = (raw[chunk, here, :] - removed) * inverse
            return carry

        lax.fori_loop(0, PARTS, finish_b, 0)

    stat_near().wait_send()
    stat_ahead().wait_send()

    def drain(chunk, carry):
        for half in range(HALVES):
            swap_copy(chunk, half).wait_send()
        for part in range(PARTS):
            back_copy(chunk, part).wait_send()
            home_copy(chunk, part).wait_send()
        return carry

    lax.fori_loop(0, chunks, drain, 0)


def per_device(view_a, view_b):
    rows, width = view_a.shape
    row_devices = lax.axis_size("row")
    groups = lax.axis_size("grp")
    bits = row_devices.bit_length() - 1
    chunks = width // LANES
    jobs = chunks // 2 + chunks
    slots = 2 * bits
    pair = 2 * LANES
    f32, bf16 = jnp.float32, jnp.bfloat16
    dma = pltpu.SemaphoreType.DMA
    anywhere = pl.BlockSpec(memory_space=pl.ANY)
    vmem = pl.BlockSpec(memory_space=pltpu.VMEM)
    grad_a, grad_b = pl.pallas_call(
        functools.partial(kernel, groups, row_devices),
        out_shape=[pltpu.VMEM((rows, width), f32)] * 2,
        in_specs=[anywhere, anywhere],
        out_specs=[vmem, vmem],
        scratch_shapes=[
            pltpu.VMEM((rows, width), bf16),
            pltpu.VMEM((rows, width), bf16),
            pltpu.VMEM((width, rows), bf16),
            pltpu.VMEM((width, rows), bf16),
            pltpu.VMEM((3 * chunks, rows, LANES), f32),
            pltpu.VMEM((chunks, rows, LANES), f32),
            pltpu.VMEM((chunks, rows, LANES), f32),
            pltpu.VMEM((chunks, rows, LANES), f32),
            pltpu.VMEM((slots, width, pair), f32),
            pltpu.VMEM((2, width // 2, pair), f32),
            pltpu.VMEM((width // 2, pair), f32),
            [pltpu.VMEM((slots, width >> (b + 1), pair), f32) for b in range(bits)],
            pltpu.VMEM((rows, pair), bf16),
            pltpu.VMEM((rows, pair), bf16),
            pltpu.VMEM((width, pair), bf16),
            pltpu.VMEM((width, pair), bf16),
            pltpu.VMEM((3 * chunks, SUBLANES, LANES), f32),
            pltpu.VMEM((3, bits + 1, SUBLANES, width), f32),
            pltpu.VMEM((3, bits, SUBLANES, width), f32),
            dma((chunks, HALVES)),
            dma((chunks, HALVES)),
            dma((chunks, HALVES)),
            dma((chunks, HALVES)),
            dma((chunks, PARTS)),
            dma((chunks, PARTS)),
            dma((chunks, PARTS)),
            dma((chunks, PARTS)),
            dma((bits, jobs)),
            dma((bits, jobs)),
            dma((bits, jobs)),
            dma((bits, jobs)),
            dma((4,)),
            dma((3, bits)),
            dma((3, bits)),
            dma((1 + chunks,)),
        ],
        compiler_params=pltpu.CompilerParams(
            collective_id=0, has_side_effects=True, vmem_limit_bytes=VMEM_LIMIT
        ),
        name="twins",
    )(view_a, view_b)

    return grad_a, grad_b


def solution(mesh):
    placed = (P("row", "grp"), P("row", "grp"))
    return jax.shard_map(
        per_device, mesh=mesh, in_specs=placed, out_specs=placed, check_vma=False
    )
```

```python
import functools

import jax
import jax.numpy as jnp
from jax import lax
from jax.experimental import pallas as pl
from jax.experimental.pallas import tpu as pltpu
from jax.sharding import PartitionSpec as P

epsilon = 1e-05
off_weight = 0.0051
LANES = 128
SUBLANES = 8
HALVES = 2
PARTS = 2
BLOCK = 256
VMEM_LIMIT = 50 << 20
HOLD = 2
WINDOW = 1
BACK_AT = 2
HOME_AT = 3
MESH = pl.DeviceIdType.MESH


def split(block):
    high = block.astype(jnp.bfloat16)
    return high, (block - high.astype(jnp.float32)).astype(jnp.bfloat16)


def dot3(left_high, left_low, right_high, right_low, contract):
    def one(left, right):
        return lax.dot_general(
            left, right, (contract, ((), ())), preferred_element_type=jnp.float32
        )

    cross = one(left_high, right_low) + one(left_low, right_high)
    return cross + one(left_high, right_high)


def kernel(
    groups,
    row_devices,
    view_a,
    view_b,
    ga,
    gb_out,
    a_high,
    a_low,
    at_high,
    at_low,
    raw,
    own_raw,
    back_in,
    swap_in,
    pen,
    share_send,
    share_kept,
    share_in,
    block_high,
    block_low,
    pen_high,
    pen_low,
    stats,
    sums,
    sums_in,
    swap_send_sem,
    swap_recv_sem,
    hop_send_sem,
    hop_recv_sem,
    back_send_sem,
    back_recv_sem,
    home_send_sem,
    home_recv_sem,
    share_send_sem,
    share_recv_sem,
    pen_send_sem,
    pen_recv_sem,
    stat_sem,
    sums_send_sem,
    sums_recv_sem,
    load_sem,
    last_in,
    last_send_sem,
    last_recv_sem,
):
    rows, width = a_high.shape
    chunks = width // LANES
    own_jobs = chunks // 2
    jobs = own_jobs + chunks
    bits = row_devices.bit_length() - 1
    slots = 2 * bits
    delay = 2 * bits - 1
    hold = max(chunks - HOLD, delay + 1)
    batch = rows * row_devices
    pair = 2 * LANES
    half_rows = rows // HALVES
    part_rows = rows // PARTS

    group = lax.axis_index("grp")
    row = lax.axis_index("row")
    sign = 1 - 2 * lax.rem(group, 2)
    near = (group + sign, row)
    ahead = (lax.rem(group + groups + 2 * sign, groups), row)
    behind = (lax.rem(group + groups - 2 * sign, groups), row)
    digit = [lax.rem(lax.div(row, 1 << b), 2) for b in range(bits)]
    peer = [(group, row + (1 - 2 * digit[b]) * (1 << b)) for b in range(bits)]
    size = [width >> (b + 1) for b in range(bits)]
    start = [0]
    for b in range(bits):
        start.append(start[b] + digit[b] * size[b])
    away = [start[b] + (1 - digit[b]) * size[b] for b in range(bits)]
    share = size[-1]

    barrier = pltpu.get_barrier_semaphore()
    others = [(group, lax.rem(row + d, row_devices)) for d in range(1, row_devices)]
    for device in [near, ahead, behind] + others:
        pl.semaphore_signal(barrier, inc=1, device_id=device, device_id_type=MESH)
    pl.semaphore_wait(barrier, 3 + len(others))

    def remote(source, target, send, recv, device):
        return pltpu.make_async_remote_copy(
            src_ref=source,
            dst_ref=target,
            send_sem=send,
            recv_sem=recv,
            device_id=device,
            device_id_type=MESH,
        )

    def lanes_of(chunk):
        return pl.ds(pl.multiple_of(chunk * LANES, LANES), LANES)

    def swap_copy(chunk, half):
        at = pl.ds(half * half_rows, half_rows)
        return remote(
            view_b.at[at, lanes_of(chunk)],
            raw.at[chunks + chunk, at, :],
            swap_send_sem.at[chunk, half],
            swap_recv_sem.at[chunk, half],
            near,
        )

    def hop_copy(chunk, half):
        at = pl.ds(half * half_rows, half_rows)
        return remote(
            raw.at[chunks + chunk, at, :],
            raw.at[2 * chunks + chunk, at, :],
            hop_send_sem.at[chunk, half],
            hop_recv_sem.at[chunk, half],
            ahead,
        )

    def back_copy(chunk, part):
        at = pl.ds(pl.multiple_of(part * part_rows, part_rows), part_rows)
        return remote(
            raw.at[2 * chunks + chunk, at, :],
            back_in.at[chunk, at, :],
            back_send_sem.at[chunk, part],
            back_recv_sem.at[chunk, part],
            behind,
        )

    def home_copy(chunk, part):
        at = pl.ds(pl.multiple_of(part * part_rows, part_rows), part_rows)
        return remote(
            raw.at[chunks + chunk, at, :],
            swap_in.at[chunk, at, :],
            home_send_sem.at[chunk, part],
            home_recv_sem.at[chunk, part],
            near,
        )

    def share_copy(job, b):
        if b == 0:
            source = share_send.at[lax.rem(job, 2)]
        else:
            at = pl.ds(pl.multiple_of(away[b] - start[b], size[b]), size[b])
            source = share_in[b - 1].at[lax.rem(job, slots), at, :]
        return remote(
            source,
            share_in[b].at[lax.rem(job, slots)],
            share_send_sem.at[b, job],
            share_recv_sem.at[b, job],
            peer[b],
        )

    def pen_copy(job, b):
        at = pl.ds(pl.multiple_of(start[b + 1], size[b]), size[b])
        return remote(
            pen.at[lax.rem(job, slots), at, :],
            pen.at[lax.rem(job, slots), at, :],
            pen_send_sem.at[b, job],
            pen_recv_sem.at[b, job],
            peer[b],
        )

    def sums_copy(which, b):
        return remote(
            sums.at[which, b],
            sums_in.at[which, b],
            sums_send_sem.at[which, b],
            sums_recv_sem.at[which, b],
            peer[b],
        )

    def all_sums(which):
        for b in range(bits):
            sums_copy(which, b).start()
            sums_copy(which, b).wait()
            sums[which, b + 1] = sums[which, b] + sums_in[which, b]
        return sums[which, bits]

    def stat_near():
        return remote(
            stats.at[pl.ds(0, chunks)],
            stats.at[pl.ds(chunks, chunks)],
            stat_sem.at[0],
            stat_sem.at[1],
            near,
        )

    def stat_ahead():
        return remote(
            stats.at[pl.ds(chunks, chunks)],
            stats.at[pl.ds(2 * chunks, chunks)],
            stat_sem.at[2],
            stat_sem.at[3],
            ahead,
        )

    swap_copy(0, 0).start()
    load_a = pltpu.make_async_copy(view_a, ga, load_sem.at[0])
    load_a.start()

    def load_own(chunk):
        return pltpu.make_async_copy(
            view_b.at[:, lanes_of(chunk)], own_raw.at[chunk], load_sem.at[1 + chunk]
        )

    for chunk in range(chunks):
        load_own(chunk).start()
    load_a.wait()
    for half in range(1, HALVES):
        swap_copy(0, half).start()

    def folded(block):
        return jnp.sum(block.reshape(-1, SUBLANES, block.shape[-1]), axis=0)

    def add_a(step, carry):
        at = pl.ds(pl.multiple_of(step * LANES, LANES), LANES)
        block = ga[at, :]
        return carry[0] + folded(block), carry[1] + folded(block * block)

    zero = jnp.zeros((SUBLANES, width), jnp.float32)
    def relay(chunk, half):
        swap_copy(chunk, half).wait_recv()
        hop_copy(chunk, half).start()

        @pl.when(chunk + WINDOW < chunks)
        def _():
            swap_copy(chunk + WINDOW, half).start()

    first, second = lax.fori_loop(0, rows // LANES, add_a, (zero, zero))
    sums[0, 0] = zero
    sums[0, 0, 0:1, :] = jnp.sum(first, axis=0, keepdims=True)
    sums[0, 0, 1:2, :] = jnp.sum(second, axis=0, keepdims=True)
    for chunk in range(chunks):
        load_own(chunk).wait()
        block = own_raw[chunk]
        raw[chunk] = block
        at = pl.ds(chunk * LANES, LANES)
        sums[0, 0, 2:3, at] = jnp.sum(folded(block), axis=0, keepdims=True)
        sums[0, 0, 3:4, at] = jnp.sum(folded(block * block), axis=0, keepdims=True)

    for chunk in range(1, WINDOW):
        for half in range(HALVES):
            swap_copy(chunk, half).start()
    relay(0, 0)
    totals = all_sums(0)
    for half in range(1, HALVES):
        relay(0, half)

    def mean_and_inverse(total, square):
        mean = total / batch
        scale = jnp.sqrt(square / batch - mean * mean + epsilon)
        return mean, 1.0 / scale

    mean_a, inverse_a = mean_and_inverse(totals[0:1, :], totals[1:2, :])
    mean_b, inverse_b = mean_and_inverse(totals[2:3, :], totals[3:4, :])
    for chunk in range(chunks):
        at = slice(chunk * LANES, (chunk + 1) * LANES)
        stats[chunk] = jnp.zeros((SUBLANES, LANES), jnp.float32)
        stats[chunk, 0:1, :] = mean_b[:, at]
        stats[chunk, 1:2, :] = inverse_b[:, at]
    stat_near().start()

    def norm_a(step, carry):
        at = pl.ds(pl.multiple_of(step * LANES, LANES), LANES)
        block = (ga[at, :] - mean_a) * inverse_a
        a_high[at, :], a_low[at, :] = split(block)
        at_high[:, at], at_low[:, at] = split(block.T)
        ga[at, :] = jnp.zeros_like(block)
        return carry

    lax.fori_loop(0, rows // LANES // 2, norm_a, 0)
    lax.fori_loop(rows // LANES // 2, rows // LANES, norm_a, 0)
    stat_near().wait_recv()
    stat_ahead().start()
    def own_of(job):
        return job >= chunks, job - chunks

    def places(job):
        is_own, index = own_of(job)
        chunk = job
        first = jnp.where(is_own, 2 * index, chunks + chunk)
        second = jnp.where(is_own, 2 * index + 1, 2 * chunks + chunk)
        return first, second

    def when_pair(job, action):
        pl.when(job < chunks)(lambda: action(job))

    def load_block(job):
        for part, place in enumerate(places(job)):
            mean = stats[place, 0:1, :]
            inverse = stats[place, 1:2, :]
            high, low = split((raw[place] - mean) * inverse)
            at = slice(part * LANES, (part + 1) * LANES)
            block_high[:, at] = high
            block_low[:, at] = low

    def correlate(job):
        @pl.when(job == 0)
        def _():
            stat_ahead().wait_recv()

        def arrived(chunk):
            for half in range(HALVES):
                hop_copy(chunk, half).wait_recv()

        when_pair(job, arrived)
        load_block(job)

        def part_of(target, base):
            count = min(BLOCK, size[0])

            def body(step, carry):
                offset = pl.multiple_of(step * count, count)
                at = pl.ds(pl.multiple_of(base + offset, count), count)
                target[pl.ds(offset, count), :] = dot3(
                    at_high[at, :],
                    at_low[at, :],
                    block_high[...],
                    block_low[...],
                    ((1,), (0,)),
                ) * (1.0 / batch)
                return carry

            lax.fori_loop(0, size[0] // count, body, 0)

        part_of(share_send.at[lax.rem(job, 2)], away[0])
        share_copy(job, 0).start()
        part_of(share_kept, start[1])

    def reduce_step(job, b):
        share_copy(job, b).wait()
        slot = lax.rem(job, slots)
        if b == 0:
            kept = share_kept[...]
        else:
            at = pl.ds(pl.multiple_of(start[b + 1] - start[b], size[b]), size[b])
            kept = share_in[b - 1][slot, at, :]
        total = kept + share_in[b][slot]
        if b < bits - 1:
            share_in[b][slot] = total
            share_copy(job, b + 1).start()
            return
        shape = (share, pair)
        row_index = start[bits] + lax.broadcasted_iota(jnp.int32, shape, 0)
        is_own, index = own_of(job)
        base = jnp.where(is_own, index * pair, -width)
        column = base + lax.broadcasted_iota(jnp.int32, shape, 1)
        value = jnp.where(
            column == row_index, -2.0 * (1.0 - total), 2.0 * off_weight * total
        )
        at = pl.ds(pl.multiple_of(start[bits], share), share)
        pen[slot, at, :] = value
        pen_copy(job, bits - 1).start()

    def gather_step(job, b):
        pen_copy(job, b).wait()
        pen_copy(job, b - 1).start()

    def consume(job):
        pen_copy(job, 0).wait()
        slot = lax.rem(job, slots)
        pen_high[...], pen_low[...] = split(pen[slot])
        load_block(job)
        first, second = places(job)

        def hopped(chunk):
            for half in range(HALVES):
                hop_copy(chunk, half).wait_send()

        when_pair(job, hopped)

        def contribute(step, carry):
            at = pl.ds(pl.multiple_of(step * BLOCK, BLOCK), BLOCK)
            value = dot3(
                a_high[at, :], a_low[at, :], pen_high[...], pen_low[...], ((1,), (0,))
            )
            raw[first, at, :] = value[:, :LANES]
            raw[second, at, :] = value[:, LANES:]
            return carry

        lax.fori_loop(0, rows // BLOCK, contribute, 0)

        def accumulate(step, carry):
            at = pl.ds(pl.multiple_of(step * BLOCK, BLOCK), BLOCK)
            ga[at, :] += dot3(
                block_high[at, :],
                block_low[at, :],
                pen_high[...],
                pen_low[...],
                ((1,), (1,)),
            )
            return carry

        lax.fori_loop(0, rows // BLOCK, accumulate, 0)

    def step_of(job, k):
        if k <= bits:
            reduce_step(job, k - 1)
        else:
            gather_step(job, 2 * bits - k)

    def send_home(chunk):
        def body(part, carry):
            back_copy(chunk, part).wait_recv()
            at = pl.ds(pl.multiple_of(part * part_rows, part_rows), part_rows)
            raw[chunks + chunk, at, :] += back_in[chunk, at, :]
            home_copy(chunk, part).start()
            return carry

        lax.fori_loop(0, PARTS, body, 0)

    def tick(t, carry):
        following = t + 1
        relays = following < chunks

        @pl.when(relays)
        def _():
            relay(following, 0)

        def run(job, action):
            pl.when(jnp.logical_and(job >= 0, job < jobs))(lambda: action(job))

        turn = t - hold

        def send_back(first, last):
            for part in range(first, last):
                back_copy(turn, part).start()

        inside = jnp.logical_and(turn >= 0, turn < chunks)
        home = turn - 1
        sent = jnp.logical_and(home >= 0, home < chunks - 1)

        def backs(place):
            if place == BACK_AT:
                pl.when(inside)(lambda: send_back(0, PARTS))

        def homes(place):
            if place == HOME_AT:
                pl.when(sent)(lambda: send_home(home))

        backs(0)
        homes(0)
        run(t, correlate)
        backs(1)
        homes(1)

        @pl.when(relays)
        def _():
            for half in range(1, HALVES):
                relay(following, half)

        run(t - delay, consume)
        backs(2)
        homes(2)
        for k in range(delay, 0, -1):
            run(t - k + 1, functools.partial(step_of, k=k))
        backs(3)
        homes(3)
        return carry

    lax.fori_loop(0, max(jobs + delay, hold + chunks), tick, 0)

    def end_a(step, carry):
        at = pl.ds(pl.multiple_of(step * LANES, LANES), LANES)
        block = ga[at, :]
        return carry[0] + folded(block), carry[1] + folded(block * normed_a(at))

    def normed_a(at):
        return a_high[at, :].astype(jnp.float32) + a_low[at, :].astype(jnp.float32)

    first, second = lax.fori_loop(0, rows // LANES, end_a, (zero, zero))
    sums[1, 0] = zero
    sums[1, 0, 0:1, :] = jnp.sum(first, axis=0, keepdims=True)
    sums[1, 0, 1:2, :] = jnp.sum(second, axis=0, keepdims=True)
    sums_copy(1, 0).start()
    sums[2, 0] = zero

    def normed_b(chunk, at):
        mean = stats[chunk, 0:1, :]
        return (own_raw[chunk, at, :] - mean) * stats[chunk, 1:2, :]

    def end_b(chunk):
        def body(part, carry):
            home_copy(chunk, part).wait_recv()
            at = pl.ds(pl.multiple_of(part * part_rows, part_rows), part_rows)
            block = raw[chunk, at, :] + swap_in[chunk, at, :]
            raw[chunk, at, :] = block
            cross = folded(block * normed_b(chunk, at))
            return carry[0] + folded(block), carry[1] + cross

        small = jnp.zeros((SUBLANES, LANES), jnp.float32)
        first, second = lax.fori_loop(0, PARTS, body, (small, small))
        at = pl.ds(chunk * LANES, LANES)
        sums[2, 0, 0:1, at] = jnp.sum(first, axis=0, keepdims=True)
        sums[2, 0, 1:2, at] = jnp.sum(second, axis=0, keepdims=True)

    for chunk in range(chunks - 2):
        end_b(chunk)
    send_home(chunks - 1)
    for b in range(bits):
        if b > 0:
            sums_copy(1, b).start()
        sums_copy(1, b).wait()
        sums[1, b + 1] = sums[1, b] + sums_in[1, b]
    ends = sums[1, bits] / batch
    end_mean, end_cross = ends[0:1, :], ends[1:2, :]

    def finish_a(step, carry):
        at = pl.ds(pl.multiple_of(step * LANES, LANES), LANES)
        ga[at, :] = (ga[at, :] - end_mean - normed_a(at) * end_cross) * inverse_a
        return carry

    lax.fori_loop(0, rows // LANES, finish_a, 0)
    for chunk in range(chunks - 2, chunks):
        end_b(chunk)
    last = [
        remote(
            sums.at[2, 0],
            last_in.at[d],
            last_send_sem.at[d],
            last_recv_sem.at[d],
            device,
        )
        for d, device in enumerate(others)
    ]
    for copy in last:
        copy.start()
    total = sums[2, 0]
    for d, copy in enumerate(last):
        copy.wait_recv()
        total = total + last_in[d]
    sums[2, bits] = total
    for chunk in range(chunks):
        at = pl.ds(chunk * LANES, LANES)
        end_mean = sums[2, bits, 0:1, at] / batch
        end_cross = sums[2, bits, 1:2, at] / batch
        inverse = stats[chunk, 1:2, :]

        def finish_b(part, carry):
            here = pl.ds(pl.multiple_of(part * part_rows, part_rows), part_rows)
            removed = end_mean + normed_b(chunk, here) * end_cross
            gb_out[here, at] = (raw[chunk, here, :] - removed) * inverse
            return carry

        lax.fori_loop(0, PARTS, finish_b, 0)

    for copy in last:
        copy.wait_send()
    stat_near().wait_send()
    stat_ahead().wait_send()

    def drain(chunk, carry):
        for half in range(HALVES):
            swap_copy(chunk, half).wait_send()
        for part in range(PARTS):
            back_copy(chunk, part).wait_send()
            home_copy(chunk, part).wait_send()
        return carry

    lax.fori_loop(0, chunks, drain, 0)


def per_device(view_a, view_b):
    rows, width = view_a.shape
    row_devices = lax.axis_size("row")
    groups = lax.axis_size("grp")
    bits = row_devices.bit_length() - 1
    chunks = width // LANES
    jobs = chunks // 2 + chunks
    slots = 2 * bits
    pair = 2 * LANES
    f32, bf16 = jnp.float32, jnp.bfloat16
    dma = pltpu.SemaphoreType.DMA
    anywhere = pl.BlockSpec(memory_space=pl.ANY)
    vmem = pl.BlockSpec(memory_space=pltpu.VMEM)
    grad_a, grad_b = pl.pallas_call(
        functools.partial(kernel, groups, row_devices),
        out_shape=[pltpu.VMEM((rows, width), f32)] * 2,
        in_specs=[anywhere, anywhere],
        out_specs=[vmem, vmem],
        scratch_shapes=[
            pltpu.VMEM((rows, width), bf16),
            pltpu.VMEM((rows, width), bf16),
            pltpu.VMEM((width, rows), bf16),
            pltpu.VMEM((width, rows), bf16),
            pltpu.VMEM((3 * chunks, rows, LANES), f32),
            pltpu.VMEM((chunks, rows, LANES), f32),
            pltpu.VMEM((chunks, rows, LANES), f32),
            pltpu.VMEM((chunks, rows, LANES), f32),
            pltpu.VMEM((slots, width, pair), f32),
            pltpu.VMEM((2, width // 2, pair), f32),
            pltpu.VMEM((width // 2, pair), f32),
            [pltpu.VMEM((slots, width >> (b + 1), pair), f32) for b in range(bits)],
            pltpu.VMEM((rows, pair), bf16),
            pltpu.VMEM((rows, pair), bf16),
            pltpu.VMEM((width, pair), bf16),
            pltpu.VMEM((width, pair), bf16),
            pltpu.VMEM((3 * chunks, SUBLANES, LANES), f32),
            pltpu.VMEM((3, bits + 1, SUBLANES, width), f32),
            pltpu.VMEM((3, bits, SUBLANES, width), f32),
            dma((chunks, HALVES)),
            dma((chunks, HALVES)),
            dma((chunks, HALVES)),
            dma((chunks, HALVES)),
            dma((chunks, PARTS)),
            dma((chunks, PARTS)),
            dma((chunks, PARTS)),
            dma((chunks, PARTS)),
            dma((bits, jobs)),
            dma((bits, jobs)),
            dma((bits, jobs)),
            dma((bits, jobs)),
            dma((4,)),
            dma((3, bits)),
            dma((3, bits)),
            dma((1 + chunks,)),
            pltpu.VMEM((row_devices - 1, SUBLANES, width), f32),
            dma((row_devices - 1,)),
            dma((row_devices - 1,)),
        ],
        compiler_params=pltpu.CompilerParams(
            collective_id=0, has_side_effects=True, vmem_limit_bytes=VMEM_LIMIT
        ),
        name="twins",
    )(view_a, view_b)

    return grad_a, grad_b


def solution(mesh):
    placed = (P("row", "grp"), P("row", "grp"))
    return jax.shard_map(
        per_device, mesh=mesh, in_specs=placed, out_specs=placed, check_vma=False
    )
```

```python
import functools

import jax
import jax.numpy as jnp
from jax import lax
from jax.experimental import pallas as pl
from jax.experimental.pallas import tpu as pltpu
from jax.sharding import PartitionSpec as P

epsilon = 1e-05
off_weight = 0.0051
LANES = 128
SUBLANES = 8
HALVES = 2
PARTS = 2
BLOCK = 512
VMEM_LIMIT = 50 << 20
HOLD = 2
WINDOW = 1
BACK_AT = 2
HOME_AT = 3
MESH = pl.DeviceIdType.MESH


def split(block):
    high = block.astype(jnp.bfloat16)
    return high, (block - high.astype(jnp.float32)).astype(jnp.bfloat16)


def dot3(left_high, left_low, right_high, right_low, contract):
    def one(left, right):
        return lax.dot_general(
            left, right, (contract, ((), ())), preferred_element_type=jnp.float32
        )

    cross = one(left_high, right_low) + one(left_low, right_high)
    return cross + one(left_high, right_high)


def kernel(
    groups,
    row_devices,
    view_a,
    view_b,
    ga,
    gb_out,
    a_high,
    a_low,
    at_high,
    at_low,
    raw,
    own_raw,
    back_in,
    swap_in,
    pen,
    share_send,
    share_kept,
    share_in,
    block_high,
    block_low,
    pen_high,
    pen_low,
    stats,
    sums,
    sums_in,
    swap_send_sem,
    swap_recv_sem,
    hop_send_sem,
    hop_recv_sem,
    back_send_sem,
    back_recv_sem,
    home_send_sem,
    home_recv_sem,
    share_send_sem,
    share_recv_sem,
    pen_send_sem,
    pen_recv_sem,
    stat_sem,
    sums_send_sem,
    sums_recv_sem,
    load_sem,
    last_in,
    last_send_sem,
    last_recv_sem,
):
    rows, width = a_high.shape
    chunks = width // LANES
    own_jobs = chunks // 2
    jobs = own_jobs + chunks
    bits = row_devices.bit_length() - 1
    slots = 2 * bits
    delay = 2 * bits - 1
    hold = max(chunks - HOLD, delay + 1)
    batch = rows * row_devices
    pair = 2 * LANES
    half_rows = rows // HALVES
    part_rows = rows // PARTS

    group = lax.axis_index("grp")
    row = lax.axis_index("row")
    sign = 1 - 2 * lax.rem(group, 2)
    near = (group + sign, row)
    ahead = (lax.rem(group + groups + 2 * sign, groups), row)
    behind = (lax.rem(group + groups - 2 * sign, groups), row)
    digit = [lax.rem(lax.div(row, 1 << b), 2) for b in range(bits)]
    peer = [(group, row + (1 - 2 * digit[b]) * (1 << b)) for b in range(bits)]
    size = [width >> (b + 1) for b in range(bits)]
    start = [0]
    for b in range(bits):
        start.append(start[b] + digit[b] * size[b])
    away = [start[b] + (1 - digit[b]) * size[b] for b in range(bits)]
    share = size[-1]

    barrier = pltpu.get_barrier_semaphore()
    others = [(group, lax.rem(row + d, row_devices)) for d in range(1, row_devices)]
    for device in [near, ahead, behind] + others:
        pl.semaphore_signal(barrier, inc=1, device_id=device, device_id_type=MESH)
    pl.semaphore_wait(barrier, 3 + len(others))

    def remote(source, target, send, recv, device):
        return pltpu.make_async_remote_copy(
            src_ref=source,
            dst_ref=target,
            send_sem=send,
            recv_sem=recv,
            device_id=device,
            device_id_type=MESH,
        )

    def lanes_of(chunk):
        return pl.ds(pl.multiple_of(chunk * LANES, LANES), LANES)

    def swap_copy(chunk, half):
        at = pl.ds(half * half_rows, half_rows)
        return remote(
            view_b.at[at, lanes_of(chunk)],
            raw.at[chunks + chunk, at, :],
            swap_send_sem.at[chunk, half],
            swap_recv_sem.at[chunk, half],
            near,
        )

    def hop_copy(chunk, half):
        at = pl.ds(half * half_rows, half_rows)
        return remote(
            raw.at[chunks + chunk, at, :],
            raw.at[2 * chunks + chunk, at, :],
            hop_send_sem.at[chunk, half],
            hop_recv_sem.at[chunk, half],
            ahead,
        )

    def back_copy(chunk, part):
        at = pl.ds(pl.multiple_of(part * part_rows, part_rows), part_rows)
        return remote(
            raw.at[2 * chunks + chunk, at, :],
            back_in.at[chunk, at, :],
            back_send_sem.at[chunk, part],
            back_recv_sem.at[chunk, part],
            behind,
        )

    def home_copy(chunk, part):
        at = pl.ds(pl.multiple_of(part * part_rows, part_rows), part_rows)
        return remote(
            raw.at[chunks + chunk, at, :],
            swap_in.at[chunk, at, :],
            home_send_sem.at[chunk, part],
            home_recv_sem.at[chunk, part],
            near,
        )

    def share_copy(job, b):
        if b == 0:
            source = share_send.at[lax.rem(job, 2)]
        else:
            at = pl.ds(pl.multiple_of(away[b] - start[b], size[b]), size[b])
            source = share_in[b - 1].at[lax.rem(job, slots), at, :]
        return remote(
            source,
            share_in[b].at[lax.rem(job, slots)],
            share_send_sem.at[b, job],
            share_recv_sem.at[b, job],
            peer[b],
        )

    def pen_copy(job, b):
        at = pl.ds(pl.multiple_of(start[b + 1], size[b]), size[b])
        return remote(
            pen.at[lax.rem(job, slots), at, :],
            pen.at[lax.rem(job, slots), at, :],
            pen_send_sem.at[b, job],
            pen_recv_sem.at[b, job],
            peer[b],
        )

    def sums_copy(which, b):
        return remote(
            sums.at[which, b],
            sums_in.at[which, b],
            sums_send_sem.at[which, b],
            sums_recv_sem.at[which, b],
            peer[b],
        )

    def all_sums(which):
        for b in range(bits):
            sums_copy(which, b).start()
            sums_copy(which, b).wait()
            sums[which, b + 1] = sums[which, b] + sums_in[which, b]
        return sums[which, bits]

    def stat_near():
        return remote(
            stats.at[pl.ds(0, chunks)],
            stats.at[pl.ds(chunks, chunks)],
            stat_sem.at[0],
            stat_sem.at[1],
            near,
        )

    def stat_ahead():
        return remote(
            stats.at[pl.ds(chunks, chunks)],
            stats.at[pl.ds(2 * chunks, chunks)],
            stat_sem.at[2],
            stat_sem.at[3],
            ahead,
        )

    swap_copy(0, 0).start()
    load_a = pltpu.make_async_copy(view_a, ga, load_sem.at[0])
    load_a.start()

    def load_own(chunk):
        return pltpu.make_async_copy(
            view_b.at[:, lanes_of(chunk)], own_raw.at[chunk], load_sem.at[1 + chunk]
        )

    for chunk in range(chunks):
        load_own(chunk).start()
    load_a.wait()
    for half in range(1, HALVES):
        swap_copy(0, half).start()

    def folded(block):
        return jnp.sum(block.reshape(-1, SUBLANES, block.shape[-1]), axis=0)

    def add_a(step, carry):
        at = pl.ds(pl.multiple_of(step * LANES, LANES), LANES)
        block = ga[at, :]
        return carry[0] + folded(block), carry[1] + folded(block * block)

    zero = jnp.zeros((SUBLANES, width), jnp.float32)
    def relay(chunk, half):
        swap_copy(chunk, half).wait_recv()
        hop_copy(chunk, half).start()

        @pl.when(chunk + WINDOW < chunks)
        def _():
            swap_copy(chunk + WINDOW, half).start()

    first, second = lax.fori_loop(0, rows // LANES, add_a, (zero, zero))
    sums[0, 0] = zero
    sums[0, 0, 0:1, :] = jnp.sum(first, axis=0, keepdims=True)
    sums[0, 0, 1:2, :] = jnp.sum(second, axis=0, keepdims=True)
    for chunk in range(chunks):
        load_own(chunk).wait()
        block = own_raw[chunk]
        raw[chunk] = block
        at = pl.ds(chunk * LANES, LANES)
        sums[0, 0, 2:3, at] = jnp.sum(folded(block), axis=0, keepdims=True)
        sums[0, 0, 3:4, at] = jnp.sum(folded(block * block), axis=0, keepdims=True)

    for chunk in range(1, WINDOW):
        for half in range(HALVES):
            swap_copy(chunk, half).start()
    relay(0, 0)
    totals = all_sums(0)
    for half in range(1, HALVES):
        relay(0, half)

    def mean_and_inverse(total, square):
        mean = total / batch
        scale = jnp.sqrt(square / batch - mean * mean + epsilon)
        return mean, 1.0 / scale

    mean_a, inverse_a = mean_and_inverse(totals[0:1, :], totals[1:2, :])
    mean_b, inverse_b = mean_and_inverse(totals[2:3, :], totals[3:4, :])
    for chunk in range(chunks):
        at = slice(chunk * LANES, (chunk + 1) * LANES)
        stats[chunk] = jnp.zeros((SUBLANES, LANES), jnp.float32)
        stats[chunk, 0:1, :] = mean_b[:, at]
        stats[chunk, 1:2, :] = inverse_b[:, at]
    stat_near().start()

    def norm_a(step, carry):
        at = pl.ds(pl.multiple_of(step * LANES, LANES), LANES)
        block = (ga[at, :] - mean_a) * inverse_a
        a_high[at, :], a_low[at, :] = split(block)
        at_high[:, at], at_low[:, at] = split(block.T)
        ga[at, :] = jnp.zeros_like(block)
        return carry

    lax.fori_loop(0, rows // LANES // 2, norm_a, 0)
    lax.fori_loop(rows // LANES // 2, rows // LANES, norm_a, 0)
    stat_near().wait_recv()
    stat_ahead().start()
    def own_of(job):
        return job >= chunks, job - chunks

    def places(job):
        is_own, index = own_of(job)
        chunk = job
        first = jnp.where(is_own, 2 * index, chunks + chunk)
        second = jnp.where(is_own, 2 * index + 1, 2 * chunks + chunk)
        return first, second

    def when_pair(job, action):
        pl.when(job < chunks)(lambda: action(job))

    def load_block(job):
        for part, place in enumerate(places(job)):
            mean = stats[place, 0:1, :]
            inverse = stats[place, 1:2, :]
            high, low = split((raw[place] - mean) * inverse)
            at = slice(part * LANES, (part + 1) * LANES)
            block_high[:, at] = high
            block_low[:, at] = low

    def correlate(job):
        @pl.when(job == 0)
        def _():
            stat_ahead().wait_recv()

        def arrived(chunk):
            for half in range(HALVES):
                hop_copy(chunk, half).wait_recv()

        when_pair(job, arrived)
        load_block(job)

        def part_of(target, base):
            count = min(BLOCK, size[0])

            def body(step, carry):
                offset = pl.multiple_of(step * count, count)
                at = pl.ds(pl.multiple_of(base + offset, count), count)
                target[pl.ds(offset, count), :] = dot3(
                    at_high[at, :],
                    at_low[at, :],
                    block_high[...],
                    block_low[...],
                    ((1,), (0,)),
                ) * (1.0 / batch)
                return carry

            lax.fori_loop(0, size[0] // count, body, 0)

        part_of(share_send.at[lax.rem(job, 2)], away[0])
        share_copy(job, 0).start()
        part_of(share_kept, start[1])

    def reduce_step(job, b):
        share_copy(job, b).wait()
        slot = lax.rem(job, slots)
        if b == 0:
            kept = share_kept[...]
        else:
            at = pl.ds(pl.multiple_of(start[b + 1] - start[b], size[b]), size[b])
            kept = share_in[b - 1][slot, at, :]
        total = kept + share_in[b][slot]
        if b < bits - 1:
            share_in[b][slot] = total
            share_copy(job, b + 1).start()
            return
        shape = (share, pair)
        row_index = start[bits] + lax.broadcasted_iota(jnp.int32, shape, 0)
        is_own, index = own_of(job)
        base = jnp.where(is_own, index * pair, -width)
        column = base + lax.broadcasted_iota(jnp.int32, shape, 1)
        value = jnp.where(
            column == row_index, -2.0 * (1.0 - total), 2.0 * off_weight * total
        )
        at = pl.ds(pl.multiple_of(start[bits], share), share)
        pen[slot, at, :] = value
        pen_copy(job, bits - 1).start()

    def gather_step(job, b):
        pen_copy(job, b).wait()
        pen_copy(job, b - 1).start()

    def consume(job):
        pen_copy(job, 0).wait()
        slot = lax.rem(job, slots)
        pen_high[...], pen_low[...] = split(pen[slot])
        load_block(job)
        first, second = places(job)

        def hopped(chunk):
            for half in range(HALVES):
                hop_copy(chunk, half).wait_send()

        when_pair(job, hopped)

        def contribute(step, carry):
            at = pl.ds(pl.multiple_of(step * BLOCK, BLOCK), BLOCK)
            value = dot3(
                a_high[at, :], a_low[at, :], pen_high[...], pen_low[...], ((1,), (0,))
            )
            raw[first, at, :] = value[:, :LANES]
            raw[second, at, :] = value[:, LANES:]
            return carry

        lax.fori_loop(0, rows // BLOCK, contribute, 0)

        def accumulate(step, carry):
            at = pl.ds(pl.multiple_of(step * BLOCK, BLOCK), BLOCK)
            ga[at, :] += dot3(
                block_high[at, :],
                block_low[at, :],
                pen_high[...],
                pen_low[...],
                ((1,), (1,)),
            )
            return carry

        lax.fori_loop(0, rows // BLOCK, accumulate, 0)

    def step_of(job, k):
        if k <= bits:
            reduce_step(job, k - 1)
        else:
            gather_step(job, 2 * bits - k)

    def send_home(chunk):
        def body(part, carry):
            back_copy(chunk, part).wait_recv()
            at = pl.ds(pl.multiple_of(part * part_rows, part_rows), part_rows)
            raw[chunks + chunk, at, :] += back_in[chunk, at, :]
            home_copy(chunk, part).start()
            return carry

        lax.fori_loop(0, PARTS, body, 0)

    def tick(t, carry):
        following = t + 1
        relays = following < chunks

        @pl.when(relays)
        def _():
            relay(following, 0)

        def run(job, action):
            pl.when(jnp.logical_and(job >= 0, job < jobs))(lambda: action(job))

        turn = t - hold

        def send_back(first, last):
            for part in range(first, last):
                back_copy(turn, part).start()

        inside = jnp.logical_and(turn >= 0, turn < chunks)
        home = turn - 1
        sent = jnp.logical_and(home >= 0, home < chunks - 1)

        def backs(place):
            if place == BACK_AT:
                pl.when(inside)(lambda: send_back(0, PARTS))

        def homes(place):
            if place == HOME_AT:
                pl.when(sent)(lambda: send_home(home))

        backs(0)
        homes(0)
        run(t, correlate)
        backs(1)
        homes(1)

        @pl.when(relays)
        def _():
            for half in range(1, HALVES):
                relay(following, half)

        run(t - delay, consume)
        backs(2)
        homes(2)
        for k in range(delay, 0, -1):
            run(t - k + 1, functools.partial(step_of, k=k))
        backs(3)
        homes(3)
        return carry

    lax.fori_loop(0, max(jobs + delay, hold + chunks), tick, 0)

    def end_a(step, carry):
        at = pl.ds(pl.multiple_of(step * LANES, LANES), LANES)
        block = ga[at, :]
        return carry[0] + folded(block), carry[1] + folded(block * normed_a(at))

    def normed_a(at):
        return a_high[at, :].astype(jnp.float32) + a_low[at, :].astype(jnp.float32)

    first, second = lax.fori_loop(0, rows // LANES, end_a, (zero, zero))
    sums[1, 0] = zero
    sums[1, 0, 0:1, :] = jnp.sum(first, axis=0, keepdims=True)
    sums[1, 0, 1:2, :] = jnp.sum(second, axis=0, keepdims=True)
    sums_copy(1, 0).start()
    sums[2, 0] = zero

    def normed_b(chunk, at):
        mean = stats[chunk, 0:1, :]
        return (own_raw[chunk, at, :] - mean) * stats[chunk, 1:2, :]

    def end_b(chunk):
        def body(part, carry):
            home_copy(chunk, part).wait_recv()
            at = pl.ds(pl.multiple_of(part * part_rows, part_rows), part_rows)
            block = raw[chunk, at, :] + swap_in[chunk, at, :]
            raw[chunk, at, :] = block
            cross = folded(block * normed_b(chunk, at))
            return carry[0] + folded(block), carry[1] + cross

        small = jnp.zeros((SUBLANES, LANES), jnp.float32)
        first, second = lax.fori_loop(0, PARTS, body, (small, small))
        at = pl.ds(chunk * LANES, LANES)
        sums[2, 0, 0:1, at] = jnp.sum(first, axis=0, keepdims=True)
        sums[2, 0, 1:2, at] = jnp.sum(second, axis=0, keepdims=True)

    for chunk in range(chunks - 2):
        end_b(chunk)
    send_home(chunks - 1)
    for b in range(bits):
        if b > 0:
            sums_copy(1, b).start()
        sums_copy(1, b).wait()
        sums[1, b + 1] = sums[1, b] + sums_in[1, b]
    ends = sums[1, bits] / batch
    end_mean, end_cross = ends[0:1, :], ends[1:2, :]

    def finish_a(step, carry):
        at = pl.ds(pl.multiple_of(step * LANES, LANES), LANES)
        ga[at, :] = (ga[at, :] - end_mean - normed_a(at) * end_cross) * inverse_a
        return carry

    lax.fori_loop(0, rows // LANES, finish_a, 0)
    for chunk in range(chunks - 2, chunks):
        end_b(chunk)
    last = [
        remote(
            sums.at[2, 0],
            last_in.at[d],
            last_send_sem.at[d],
            last_recv_sem.at[d],
            device,
        )
        for d, device in enumerate(others)
    ]
    for copy in last:
        copy.start()
    total = sums[2, 0]
    for d, copy in enumerate(last):
        copy.wait_recv()
        total = total + last_in[d]
    sums[2, bits] = total
    for chunk in range(chunks):
        at = pl.ds(chunk * LANES, LANES)
        end_mean = sums[2, bits, 0:1, at] / batch
        end_cross = sums[2, bits, 1:2, at] / batch
        inverse = stats[chunk, 1:2, :]

        def finish_b(part, carry):
            here = pl.ds(pl.multiple_of(part * part_rows, part_rows), part_rows)
            removed = end_mean + normed_b(chunk, here) * end_cross
            gb_out[here, at] = (raw[chunk, here, :] - removed) * inverse
            return carry

        lax.fori_loop(0, PARTS, finish_b, 0)

    for copy in last:
        copy.wait_send()
    stat_near().wait_send()
    stat_ahead().wait_send()

    def drain(chunk, carry):
        for half in range(HALVES):
            swap_copy(chunk, half).wait_send()
        for part in range(PARTS):
            back_copy(chunk, part).wait_send()
            home_copy(chunk, part).wait_send()
        return carry

    lax.fori_loop(0, chunks, drain, 0)


def per_device(view_a, view_b):
    rows, width = view_a.shape
    row_devices = lax.axis_size("row")
    groups = lax.axis_size("grp")
    bits = row_devices.bit_length() - 1
    chunks = width // LANES
    jobs = chunks // 2 + chunks
    slots = 2 * bits
    pair = 2 * LANES
    f32, bf16 = jnp.float32, jnp.bfloat16
    dma = pltpu.SemaphoreType.DMA
    anywhere = pl.BlockSpec(memory_space=pl.ANY)
    vmem = pl.BlockSpec(memory_space=pltpu.VMEM)
    grad_a, grad_b = pl.pallas_call(
        functools.partial(kernel, groups, row_devices),
        out_shape=[pltpu.VMEM((rows, width), f32)] * 2,
        in_specs=[anywhere, anywhere],
        out_specs=[vmem, vmem],
        scratch_shapes=[
            pltpu.VMEM((rows, width), bf16),
            pltpu.VMEM((rows, width), bf16),
            pltpu.VMEM((width, rows), bf16),
            pltpu.VMEM((width, rows), bf16),
            pltpu.VMEM((3 * chunks, rows, LANES), f32),
            pltpu.VMEM((chunks, rows, LANES), f32),
            pltpu.VMEM((chunks, rows, LANES), f32),
            pltpu.VMEM((chunks, rows, LANES), f32),
            pltpu.VMEM((slots, width, pair), f32),
            pltpu.VMEM((2, width // 2, pair), f32),
            pltpu.VMEM((width // 2, pair), f32),
            [pltpu.VMEM((slots, width >> (b + 1), pair), f32) for b in range(bits)],
            pltpu.VMEM((rows, pair), bf16),
            pltpu.VMEM((rows, pair), bf16),
            pltpu.VMEM((width, pair), bf16),
            pltpu.VMEM((width, pair), bf16),
            pltpu.VMEM((3 * chunks, SUBLANES, LANES), f32),
            pltpu.VMEM((3, bits + 1, SUBLANES, width), f32),
            pltpu.VMEM((3, bits, SUBLANES, width), f32),
            dma((chunks, HALVES)),
            dma((chunks, HALVES)),
            dma((chunks, HALVES)),
            dma((chunks, HALVES)),
            dma((chunks, PARTS)),
            dma((chunks, PARTS)),
            dma((chunks, PARTS)),
            dma((chunks, PARTS)),
            dma((bits, jobs)),
            dma((bits, jobs)),
            dma((bits, jobs)),
            dma((bits, jobs)),
            dma((4,)),
            dma((3, bits)),
            dma((3, bits)),
            dma((1 + chunks,)),
            pltpu.VMEM((row_devices - 1, SUBLANES, width), f32),
            dma((row_devices - 1,)),
            dma((row_devices - 1,)),
        ],
        compiler_params=pltpu.CompilerParams(
            collective_id=0, has_side_effects=True, vmem_limit_bytes=VMEM_LIMIT
        ),
        name="twins",
    )(view_a, view_b)

    return grad_a, grad_b


def solution(mesh):
    placed = (P("row", "grp"), P("row", "grp"))
    return jax.shard_map(
        per_device, mesh=mesh, in_specs=placed, out_specs=placed, check_vma=False
    )
```
